256 devices in a mesh: section: 8 (over z), expert: 8 (over x_lo, y), mp: 4 (over x_hi, core).
Axes of the slice: x: 4 (x_hi: 2, x_lo: 2; x = x_hi * 2 + x_lo), y: 4, z: 8, core: 2. Of those that a mesh axis runs over, the one named last changes fastest.
Arguments:
- grad_in: bfloat16 [8, 1024, 3072], P('section', 'expert', 'mp'), may hold values from -6 to 6
- saved_input: bfloat16 [8, 2, 1024, 3072], P('section', None, 'expert', 'mp'), may hold values from -6 to 6
- routes: int32 [8, 2, 1024, 2], P('section', None, 'expert'), may hold values from 0 to 3, all different within a row; in each aligned block of 128 rows (0 to 127, 128 to 255, ..., all dimensions but the last counted through in order) at most 72 rows name the same one
- route_weights: float32 [8, 2, 1024, 2], P('section', None, 'expert'), may hold values from 0.2 to 1
- plan: int32 [8, 2], P('section'), may hold values from 0 to 1, each once within a row
- up_weight: bfloat16 [8, 3072, 32768], P('section', None, ('expert', 'mp')), may hold values from -0.109375 to 0.109375
- down_weight: bfloat16 [8, 32768, 3072], P('section', ('expert', 'mp')), may hold values from -0.0625 to 0.0625
Outputs:
- passed_grad: bfloat16 [8, 1024, 3072], P('section', 'expert', 'mp')
The draws below stay inside these ranges and needn't reach their ends.
Inputs may be any that keep to these rules, and one draw needn't show every extreme that they name: `routes`: the numbers of a row differ. In each aligned block of 128 rows (the rows of one index of expert within one section and microbatch) no expert is named by more than 72 rows, and some block reaches 72. `plan`: each row is a permutation of 0 to 1.
All inputs are finite; a program needn't handle non-finite values.
Results may differ from the reference program's by a relative error of at most 0.0065.
Values may be sent and summed in bfloat16 or wider, within the bound.
No kernel may reach another device: no remote copies, remote signals or barrier semaphores. Data moves between devices by JAX's collectives and lax.ppermute only.
A program may use at most 128 MiB of HBM per device.

```python
import math
import jax
import jax.numpy as jnp
import numpy as np
from jax import lax

D = 3072
FF = 8192
EXPERTS = 4
TOP = 2
MICRO = 2
ROWS_DEV = 128
CAPACITY = 72
SECTIONS = 8
GROUP_ROWS = 1024
N_EXPERT = 8


def block_levels(rng, extent, pieces, least, high):
    factor_of = 1.0
    for dim, shards_of in pieces:
        draws = jax.random.uniform(jax.random.fold_in(jax.random.fold_in(rng, 6), dim), (shards_of,), jnp.float32, least / len(pieces), high / len(pieces))
        factor_of = factor_of * jnp.repeat(jnp.exp(draws), extent[dim] // shards_of).reshape((-1,) + (1,) * (len(extent) - 1 - dim))
    return factor_of


def routed_block(stream_key, own, number, rows, count, top, reach, skew):
    ranking = jax.random.permutation(stream_key, count)
    heavy_load, common = shares(count, rows * top, reach, skew, True), shares(count, rows * top, reach, skew, False)
    places = jnp.arange(count)

    def named(tallies, rotation):
        used = int((tallies > 0).sum())
        fixed = max(1, used // 4)
        passed = fixed + (places - fixed + rotation * (used - fixed)) % max(1, count - fixed)
        return jnp.zeros((count,), jnp.int32).at[ranking[jnp.where(places < fixed, places, passed)]].set(jnp.asarray(tallies, jnp.int32))

    tallies = jnp.where(number % 4 == 0, named(heavy_load, number // 4), named(common, number - number // 4 - 1))
    mixed = jax.random.permutation(jax.random.fold_in(own, 3), count)
    giver, receiver = mixed[0:count // 2 * 2:2], mixed[1:count // 2 * 2:2]
    slack = jnp.minimum(tallies[giver] - 1, reach - tallies[receiver]) // 2
    slack = jnp.where((giver == ranking[0]) | (receiver == ranking[0]) | (tallies[receiver] == 0), 0, jnp.maximum(slack, 0))
    passed = jax.random.randint(jax.random.fold_in(own, 4), (count // 2,), 0, 1 << 20) % (slack + 1)
    tallies = tallies.at[giver].add(-passed).at[receiver].add(passed)
    items = jnp.searchsorted(jnp.cumsum(tallies), jnp.arange(rows * top), side="right").astype(jnp.int32)
    grid = items.reshape(top, rows).T
    grid = grid[jax.random.permutation(jax.random.fold_in(own, 1), rows)]
    rotation = jax.random.randint(jax.random.fold_in(own, 2), (rows, 1), 0, top)
    return jnp.take_along_axis(grid, (jnp.arange(top)[None, :] + rotation) % top, axis=1)


def shares(amount, total, most, skew, full):
    portions = [(1 << 20) // math.isqrt(rank ** skew) + 1 for rank in range(1, amount + 1)]
    largest = most if full else min(most, max(-(-total // amount), total * portions[0] // sum(portions)))
    least = 1 if total - largest >= amount - 1 else 0
    given, rest = [largest] + [least] * (amount - 1), total - largest - least * (amount - 1)
    while rest > 0:
        candidates = [i for i in range(1, amount) if given[i] < largest] or [i for i in range(1, amount) if given[i] < most]
        whole, left = sum([portions[i] for i in candidates]), rest
        for i in candidates:
            more = min(most - given[i], max(1, left * portions[i] // whole), rest)
            given[i] = given[i] + more
            rest = rest - more
    return np.array(given)


def centred(stream_key, dims, width, reach, cuts=(), kind=jnp.bfloat16):
    values = jax.random.normal(stream_key, dims, jnp.float32) * width
    if len(cuts) > 0:
        values = block_levels(stream_key, dims, cuts, -0.22, 0.18) * values
    return jnp.clip(values, min=-reach, max=reach).astype(kind)


def setup_inputs(seed: int = 0) -> dict:
    arg_keys = jax.random.split(jax.random.key(seed), 8)
    grad_in = centred(arg_keys[0], (SECTIONS, GROUP_ROWS, D), 1.0, 6.0, ((0, 8), (1, 8), (2, 4)))
    saved_input = centred(arg_keys[1], (SECTIONS, MICRO, GROUP_ROWS, D), 1.0, 6.0, ((0, 8), (2, 8), (3, 4)))
    routes_keys = jax.random.split(jax.random.fold_in(arg_keys[2], 1), SECTIONS * MICRO * GROUP_ROWS // ROWS_DEV)
    routes_turns = jax.random.permutation(jax.random.fold_in(arg_keys[2], 3), SECTIONS * MICRO * GROUP_ROWS // ROWS_DEV)
    routes = jax.vmap(lambda own, number: routed_block(jax.random.fold_in(arg_keys[2], 2), own, number, ROWS_DEV, EXPERTS, TOP, CAPACITY, 2))(routes_keys, routes_turns).reshape((SECTIONS, MICRO, GROUP_ROWS, TOP))
    route_weights = jnp.clip(0.2 + 0.8 * jax.random.uniform(arg_keys[3], (SECTIONS, MICRO, GROUP_ROWS, TOP), jnp.float32) ** block_levels(arg_keys[3], (SECTIONS, MICRO, GROUP_ROWS, TOP), ((0, 8), (2, 8)), -0.2, 0.2), 0.2, 1.0)
    plan = jax.vmap(lambda own: jax.random.permutation(own, MICRO))(jax.random.split(arg_keys[4], SECTIONS)).reshape((SECTIONS, MICRO)).astype(jnp.int32)
    up_weight = centred(arg_keys[5], (SECTIONS, D, EXPERTS * FF), D ** -0.5, 0.109375, ((0, 8), (2, 32)))
    down_weight = centred(arg_keys[6], (SECTIONS, EXPERTS * FF, D), FF ** -0.5, 0.0625, ((0, 8), (1, 32)))
    return {"grad_in": grad_in, "saved_input": saved_input, "routes": routes, "route_weights": route_weights, "plan": plan, "up_weight": up_weight, "down_weight": down_weight}


def slot_targets(route_now):
    blocks = route_now.reshape(N_EXPERT, ROWS_DEV, TOP)
    expert_ids = jnp.arange(EXPERTS, dtype=jnp.int32)
    onehot = (blocks[..., None] == expert_ids).astype(jnp.int32)
    counts = jnp.sum(onehot, axis=2)
    before = jnp.cumsum(counts, axis=1) - counts
    slot_pos = jnp.sum(before[:, :, None, :] * onehot, axis=3)
    return (blocks * CAPACITY + slot_pos).astype(jnp.int32)


def expert_back(operands):
    expert_id, rows_in, grads_in, up_all, down_all = operands
    start = (expert_id * FF).astype(jnp.int32)
    up_cols = lax.dynamic_slice_in_dim(up_all, start, FF, 1)
    down_rows = lax.dynamic_slice_in_dim(down_all, start, FF, 0)
    pre_act = jnp.dot(rows_in, up_cols, preferred_element_type=jnp.float32)
    grad_act = jnp.dot(grads_in, down_rows.T, preferred_element_type=jnp.float32)
    sigma_up = jax.nn.sigmoid(pre_act)
    grad_pre = (grad_act * sigma_up * (1.0 + pre_act * (1.0 - sigma_up))).astype(jnp.bfloat16)
    return jnp.dot(grad_pre, up_cols.T, preferred_element_type=jnp.float32)


def layer_back(grad_rows, saved_rows, route_now, weight_now, up_all, down_all):
    target = slot_targets(route_now)
    group_ids = jnp.broadcast_to(jnp.arange(N_EXPERT, dtype=jnp.int32)[:, None, None], target.shape)
    saved_blocks = saved_rows.reshape(N_EXPERT, ROWS_DEV, D)
    grad_blocks = grad_rows.reshape(N_EXPERT, ROWS_DEV, D)
    saved_rep = jnp.broadcast_to(saved_blocks[:, :, None, :], (N_EXPERT, ROWS_DEV, TOP, D))
    grad_rep = jnp.broadcast_to(grad_blocks[:, :, None, :], (N_EXPERT, ROWS_DEV, TOP, D))
    buffer_in = jnp.zeros((N_EXPERT, EXPERTS * CAPACITY, D), jnp.bfloat16).at[group_ids, target].set(saved_rep)
    buffer_grad = jnp.zeros((N_EXPERT, EXPERTS * CAPACITY, D), jnp.bfloat16).at[group_ids, target].set(grad_rep)

    def by_expert(buffer):
        return buffer.reshape(N_EXPERT, EXPERTS, CAPACITY, D).transpose(1, 0, 2, 3).reshape(EXPERTS, N_EXPERT * CAPACITY, D)

    def one_expert(operands):
        expert_id, rows_in, grads_in = operands
        return expert_back((expert_id, rows_in, grads_in, up_all, down_all))

    branch = lax.map(one_expert, (jnp.arange(EXPERTS, dtype=jnp.int32), by_expert(buffer_in), by_expert(buffer_grad)))
    branch = branch.reshape(EXPERTS, N_EXPERT, CAPACITY, D).transpose(1, 0, 2, 3).reshape(N_EXPERT, EXPERTS * CAPACITY, D)
    picked = branch[group_ids, target]
    weights_blk = weight_now.reshape(N_EXPERT, ROWS_DEV, TOP)
    mixed = jnp.sum(weights_blk[..., None] * picked, axis=2)
    return (grad_blocks.astype(jnp.float32) + mixed).astype(jnp.bfloat16).reshape(GROUP_ROWS, D)


def run_tick(grads, micro_ids, saved_input, routes, route_weights, up_weight, down_weight):
    def section_back(operands):
        grad_rows, saved_s, routes_s, weights_s, micro_index, up_all, down_all = operands

        def select_micro(array):
            return lax.dynamic_index_in_dim(array, micro_index, 0, keepdims=False)

        return layer_back(grad_rows, select_micro(saved_s), select_micro(routes_s), select_micro(weights_s), up_all, down_all)

    return lax.map(section_back, (grads, saved_input, routes, route_weights, micro_ids, up_weight, down_weight))


def reference(grad_in, saved_input, routes, route_weights, plan, up_weight, down_weight):
    first = run_tick(grad_in, plan[:, 0], saved_input, routes, route_weights, up_weight, down_weight)
    second = run_tick(jnp.roll(first, -1, axis=0), plan[:, 1], saved_input, routes, route_weights, up_weight, down_weight)
    return jnp.roll(second, -1, axis=0)
```

```python
import jax
import jax.numpy as jnp
from jax import lax
from jax.experimental import pallas as pl
from jax.experimental.pallas import tpu as pltpu
from jax.sharding import Mesh, PartitionSpec as P

EXPERTS = 4
CAPACITY = 72
HIDDEN_BLOCK = 256
VMEM_LIMIT = 48 * 1024 * 1024


def contract_last(left, right):
    return lax.dot_general(
        left, right, (((1,), (1,)), ((), ())), preferred_element_type=jnp.float32
    )


def factor_kernel(core_ref, mine_ref, other_ref, up_ref, factor_ref):
    core = core_ref[0]
    quarter = mine_ref.shape[2]
    pre = None
    for xhi in range(mine_ref.shape[0]):
        own = pl.multiple_of((2 * xhi + core) * quarter, quarter)
        theirs = pl.multiple_of((2 * xhi + 1 - core) * quarter, quarter)
        part = jnp.dot(
            mine_ref[xhi], up_ref[pl.ds(own, quarter), :], preferred_element_type=jnp.float32
        ) + jnp.dot(
            other_ref[xhi], up_ref[pl.ds(theirs, quarter), :], preferred_element_type=jnp.float32
        )
        pre = part if pre is None else pre + part
    sigma = jax.nn.sigmoid(pre)
    factor_ref[...] = sigma * (1.0 + pre * (1.0 - sigma))


def factor(core, mine, other, up):
    halves, rows, quarter = mine.shape
    width, hidden = up.shape
    whole = pl.BlockSpec((halves, rows, quarter), lambda i, c: (0, 0, 0))
    return pl.pallas_call(
        factor_kernel,
        out_shape=jax.ShapeDtypeStruct((rows, hidden), jnp.float32),
        grid_spec=pltpu.PrefetchScalarGridSpec(
            num_scalar_prefetch=1,
            grid=(hidden // HIDDEN_BLOCK,),
            in_specs=[whole, whole, pl.BlockSpec((width, HIDDEN_BLOCK), lambda i, c: (0, i))],
            out_specs=pl.BlockSpec((rows, HIDDEN_BLOCK), lambda i, c: (0, i)),
        ),
        compiler_params=pltpu.CompilerParams(
            dimension_semantics=("arbitrary",), vmem_limit_bytes=VMEM_LIMIT
        ),
        name="factor",
    )(core, mine, other, up)


def branch_kernel(
    core_ref, mine_ref, other_ref, down_ref, factor_ref, up_ref, send_ref, keep_ref, grad_pre
):
    core = core_ref[0]
    step = pl.program_id(0)
    halves, _, quarter = mine_ref.shape
    blocks = grad_pre.shape[0]

    @pl.when(step < blocks)
    def _():
        act = None
        for xhi in range(halves):
            own = pl.multiple_of((2 * xhi + core) * quarter, quarter)
            theirs = pl.multiple_of((2 * xhi + 1 - core) * quarter, quarter)
            part = contract_last(mine_ref[xhi], down_ref[:, pl.ds(own, quarter)]) + contract_last(
                other_ref[xhi], down_ref[:, pl.ds(theirs, quarter)]
            )
            act = part if act is None else act + part
        grad_pre[step] = (act * factor_ref[...]).astype(jnp.bfloat16)

    def partial():
        total = None
        for block in range(blocks):
            part = contract_last(
                grad_pre[block], up_ref[:, block * HIDDEN_BLOCK : (block + 1) * HIDDEN_BLOCK]
            )
            total = part if total is None else total + part
        return total.astype(jnp.bfloat16)

    @pl.when((step >= blocks) & (step < blocks + halves))
    def _():
        send_ref[0] = partial()

    @pl.when(step >= blocks + halves)
    def _():
        keep_ref[0] = partial()


def branch(core, mine, other, down, factors, up):
    halves, rows, quarter = mine.shape
    hidden, width = down.shape
    blocks = hidden // HIDDEN_BLOCK
    whole = pl.BlockSpec((halves, rows, quarter), lambda i, c: (0, 0, 0))

    def hidden_block(i):
        return jnp.minimum(i, blocks - 1)

    def up_block(i, c):
        late = jnp.maximum(i - blocks, 0)
        half = late % halves
        side = jnp.where(late < halves, 1 - c[0], c[0])
        return (2 * half + side, 0)

    out = jax.ShapeDtypeStruct((halves, rows, quarter), jnp.bfloat16)
    return pl.pallas_call(
        branch_kernel,
        out_shape=(out, out),
        grid_spec=pltpu.PrefetchScalarGridSpec(
            num_scalar_prefetch=1,
            grid=(blocks + 2 * halves,),
            in_specs=[
                whole,
                whole,
                pl.BlockSpec((HIDDEN_BLOCK, width), lambda i, c: (hidden_block(i), 0)),
                pl.BlockSpec((rows, HIDDEN_BLOCK), lambda i, c: (0, hidden_block(i))),
                pl.BlockSpec((quarter, hidden), up_block),
            ],
            out_specs=(
                pl.BlockSpec(
                    (1, rows, quarter), lambda i, c: (jnp.clip(i - blocks, 0, halves - 1), 0, 0)
                ),
                pl.BlockSpec(
                    (1, rows, quarter),
                    lambda i, c: (jnp.clip(i - blocks - halves, 0, halves - 1), 0, 0),
                ),
            ),
            scratch_shapes=[pltpu.VMEM((blocks, rows, HIDDEN_BLOCK), jnp.bfloat16)],
        ),
        compiler_params=pltpu.CompilerParams(
            dimension_semantics=("arbitrary",), vmem_limit_bytes=VMEM_LIMIT
        ),
        name="branch",
    )(core, mine, other, down, factors, up)


def slots(route_now, share_now):
    rows = route_now.shape[0]
    named = route_now.T[None] == jnp.arange(EXPERTS, dtype=jnp.int32)[:, None, None]
    chosen = jnp.any(named, axis=1)
    mix = jnp.sum(jnp.where(named, share_now.T[None], 0.0), axis=1)
    token = jnp.arange(rows, dtype=jnp.int32)
    earlier = (token[:, None] < token[None, :]).astype(jnp.bfloat16)
    before = jnp.dot(
        chosen.astype(jnp.bfloat16), earlier, preferred_element_type=jnp.float32
    ).astype(jnp.int32)
    place = jnp.where(chosen, before, -1)
    hit = place[:, None, :] == jnp.arange(CAPACITY, dtype=jnp.int32)[None, :, None]
    mixing = jnp.where(hit, mix[:, None, :], 0.0).reshape(EXPERTS * CAPACITY, rows)
    return hit, mixing


def per_device(grad_in, saved_input, routes, route_weights, plan, up_weight, down_weight):
    n_expert = lax.axis_size("expert")
    n_xhi = lax.axis_size("xhi")
    n_section = lax.axis_size("section")
    per_expert = n_expert // EXPERTS
    peers = n_xhi * n_expert
    rows, quarter = grad_in.shape[1:]
    up_local = up_weight[0]
    down_local = down_weight[0]
    core = lax.axis_index("core").astype(jnp.int32).reshape(1)

    def swap_cores(value):
        return lax.ppermute(value, "core", [(0, 1), (1, 0)])

    def exchange(value):
        return lax.all_to_all(value, ("xhi", "expert"), split_axis=0, concat_axis=0, tiled=True)

    def dispatch(hit, value):
        select = jnp.broadcast_to(
            hit[None, :, None], (n_xhi, EXPERTS, per_expert, CAPACITY, rows)
        ).reshape(peers * CAPACITY, rows)
        sent = jnp.dot(
            select.astype(jnp.bfloat16), value, preferred_element_type=jnp.float32
        ).astype(jnp.bfloat16)
        got = exchange(sent.reshape(peers, CAPACITY, quarter))
        mine = got.reshape(n_xhi, n_expert * CAPACITY, quarter)
        return mine, swap_cores(mine)

    ticks = []
    for step_index in range(plan.shape[1]):
        micro = plan[0, step_index]
        saved_now = lax.dynamic_index_in_dim(saved_input[0], micro, 0, keepdims=False)
        route_now = lax.dynamic_index_in_dim(routes[0], micro, 0, keepdims=False)
        share_now = lax.dynamic_index_in_dim(route_weights[0], micro, 0, keepdims=False)
        hit, mixing = slots(route_now, share_now)
        ticks.append((saved_now, hit, mixing))

    current = grad_in[0]
    for saved_now, hit, mixing in ticks:
        factors = factor(core, *dispatch(hit, saved_now), up_local)
        send, keep = branch(core, *dispatch(hit, current), down_local, factors, up_local)
        outgoing = (
            keep.astype(jnp.float32) + swap_cores(send).astype(jnp.float32)
        ).astype(jnp.bfloat16)
        arrived = exchange(outgoing.reshape(peers, CAPACITY, quarter))
        summed = jnp.sum(
            arrived.reshape(n_xhi, EXPERTS, per_expert, CAPACITY, quarter).astype(jnp.float32),
            axis=(0, 2),
        )
        moe_term = lax.dot_general(
            mixing,
            summed.reshape(EXPERTS * CAPACITY, quarter),
            (((0,), (0,)), ((), ())),
            precision=lax.Precision.HIGHEST,
            preferred_element_type=jnp.float32,
        )
        result = (current.astype(jnp.float32) + moe_term).astype(jnp.bfloat16)
        current = lax.ppermute(
            result, "section", [(i, (i - 1) % n_section) for i in range(n_section)]
        )
    return current[None]


def solution(mesh):
    sections, experts, parts = (mesh.shape[name] for name in ("section", "expert", "mp"))
    refined = Mesh(
        mesh.devices.reshape(sections, experts, parts // 2, 2),
        ("section", "expert", "xhi", "core"),
    )
    mp = ("xhi", "core")
    placed = (
        P("section", "expert", mp),
        P("section", None, "expert", mp),
        P("section", None, "expert", None),
        P("section", None, "expert", None),
        P("section", None),
        P("section", None, ("expert", "xhi", "core")),
        P("section", ("expert", "xhi", "core"), None),
    )
    return jax.shard_map(
        per_device,
        mesh=refined,
        in_specs=placed,
        out_specs=P("section", "expert", mp),
        check_vma=False,
    )
```

```python
import jax
import jax.numpy as jnp
from jax import lax
from jax.experimental import pallas as pl
from jax.experimental.pallas import tpu as pltpu
from jax.sharding import Mesh, PartitionSpec as P

EXPERTS = 4
CAPACITY = 72
HIDDEN_BLOCK = 256
VMEM_LIMIT = 32 * 1024 * 1024


def together(*values):
    return lax.optimization_barrier(values)


def contract_last(left, right):
    return lax.dot_general(
        left, right, (((1,), (1,)), ((), ())), preferred_element_type=jnp.float32
    )


def factor_kernel(core_ref, mine_ref, other_ref, up_ref, factor_ref):
    core = core_ref[0]
    quarter = mine_ref.shape[2]
    pre = None
    for xhi in range(mine_ref.shape[0]):
        own = pl.multiple_of((2 * xhi + core) * quarter, quarter)
        theirs = pl.multiple_of((2 * xhi + 1 - core) * quarter, quarter)
        part = jnp.dot(
            mine_ref[xhi], up_ref[pl.ds(own, quarter), :], preferred_element_type=jnp.float32
        ) + jnp.dot(
            other_ref[xhi], up_ref[pl.ds(theirs, quarter), :], preferred_element_type=jnp.float32
        )
        pre = part if pre is None else pre + part
    sigma = jax.nn.sigmoid(pre)
    factor_ref[...] = sigma * (1.0 + pre * (1.0 - sigma))


def factor(core, mine, other, up):
    halves, rows, quarter = mine.shape
    width, hidden = up.shape
    whole = pl.BlockSpec((halves, rows, quarter), lambda i, c: (0, 0, 0))
    return pl.pallas_call(
        factor_kernel,
        out_shape=pltpu.HBM((rows, hidden), jnp.float32),
        grid_spec=pltpu.PrefetchScalarGridSpec(
            num_scalar_prefetch=1,
            grid=(hidden // HIDDEN_BLOCK,),
            in_specs=[whole, whole, pl.BlockSpec((width, HIDDEN_BLOCK), lambda i, c: (0, i))],
            out_specs=pl.BlockSpec((rows, HIDDEN_BLOCK), lambda i, c: (0, i)),
        ),
        compiler_params=pltpu.CompilerParams(
            dimension_semantics=("arbitrary",), vmem_limit_bytes=VMEM_LIMIT
        ),
        cost_estimate=pl.CostEstimate(
            flops=2 * rows * width * hidden,
            transcendentals=2 * rows * hidden,
            bytes_accessed=2 * width * (rows + hidden) + 4 * rows * hidden,
        ),
        name="factor",
    )(core, mine, other, up)


def branch_kernel(
    core_ref, mine_ref, other_ref, down_ref, factor_ref, up_ref, send_ref, keep_ref, grad_pre
):
    core = core_ref[0]
    step = pl.program_id(0)
    halves, _, quarter = mine_ref.shape
    blocks = grad_pre.shape[0]

    @pl.when(step < blocks)
    def _():
        act = None
        for xhi in range(halves):
            own = pl.multiple_of((2 * xhi + core) * quarter, quarter)
            theirs = pl.multiple_of((2 * xhi + 1 - core) * quarter, quarter)
            part = contract_last(mine_ref[xhi], down_ref[:, pl.ds(own, quarter)]) + contract_last(
                other_ref[xhi], down_ref[:, pl.ds(theirs, quarter)]
            )
            act = part if act is None else act + part
        grad_pre[step] = (act * factor_ref[...]).astype(jnp.bfloat16)

    def partial():
        total = None
        for block in range(blocks):
            part = contract_last(
                grad_pre[block], up_ref[:, block * HIDDEN_BLOCK : (block + 1) * HIDDEN_BLOCK]
            )
            total = part if total is None else total + part
        return total.astype(jnp.bfloat16)

    @pl.when((step >= blocks) & (step < blocks + halves))
    def _():
        send_ref[0] = partial()

    @pl.when(step >= blocks + halves)
    def _():
        keep_ref[0] = partial()


def branch(core, mine, other, down, factors, up):
    halves, rows, quarter = mine.shape
    hidden, width = down.shape
    blocks = hidden // HIDDEN_BLOCK
    whole = pl.BlockSpec((halves, rows, quarter), lambda i, c: (0, 0, 0))

    def hidden_block(i):
        return jnp.minimum(i, blocks - 1)

    def up_block(i, c):
        late = jnp.maximum(i - blocks, 0)
        half = late % halves
        side = jnp.where(late < halves, 1 - c[0], c[0])
        return (2 * half + side, 0)

    out = jax.ShapeDtypeStruct((halves, rows, quarter), jnp.bfloat16)
    return pl.pallas_call(
        branch_kernel,
        out_shape=(out, out),
        grid_spec=pltpu.PrefetchScalarGridSpec(
            num_scalar_prefetch=1,
            grid=(blocks + 2 * halves,),
            in_specs=[
                whole,
                whole,
                pl.BlockSpec((HIDDEN_BLOCK, width), lambda i, c: (hidden_block(i), 0)),
                pl.BlockSpec((rows, HIDDEN_BLOCK), lambda i, c: (0, hidden_block(i))),
                pl.BlockSpec((quarter, hidden), up_block),
            ],
            out_specs=(
                pl.BlockSpec(
                    (1, rows, quarter), lambda i, c: (jnp.clip(i - blocks, 0, halves - 1), 0, 0)
                ),
                pl.BlockSpec(
                    (1, rows, quarter),
                    lambda i, c: (jnp.clip(i - blocks - halves, 0, halves - 1), 0, 0),
                ),
            ),
            scratch_shapes=[pltpu.VMEM((blocks, rows, HIDDEN_BLOCK), jnp.bfloat16)],
        ),
        compiler_params=pltpu.CompilerParams(
            dimension_semantics=("arbitrary",), vmem_limit_bytes=VMEM_LIMIT
        ),
        cost_estimate=pl.CostEstimate(
            flops=4 * rows * hidden,
            transcendentals=0,
            bytes_accessed=4 * rows * hidden,
        ),
        name="branch",
    )(core, mine, other, down, factors, up)


def slots(route_now, share_now):
    rows = route_now.shape[0]
    named = route_now.T[None] == jnp.arange(EXPERTS, dtype=jnp.int32)[:, None, None]
    chosen = jnp.any(named, axis=1)
    mix = jnp.sum(jnp.where(named, share_now.T[None], 0.0), axis=1)
    token = jnp.arange(rows, dtype=jnp.int32)
    earlier = (token[:, None] < token[None, :]).astype(jnp.bfloat16)
    before = jnp.dot(
        chosen.astype(jnp.bfloat16), earlier, preferred_element_type=jnp.float32
    ).astype(jnp.int32)
    place = jnp.where(chosen, before, -1)
    hit = place[:, None, :] == jnp.arange(CAPACITY, dtype=jnp.int32)[None, :, None]
    mixing = jnp.where(hit, mix[:, None, :], 0.0).reshape(EXPERTS * CAPACITY, rows)
    return hit, mixing


def per_device(grad_in, saved_input, routes, route_weights, plan, up_weight, down_weight):
    n_expert = lax.axis_size("expert")
    n_xhi = lax.axis_size("xhi")
    n_section = lax.axis_size("section")
    per_expert = n_expert // EXPERTS
    peers = n_xhi * n_expert
    rows, quarter = grad_in.shape[1:]
    up_local = pltpu.with_memory_space_constraint(up_weight[0], pltpu.HBM)
    down_local = pltpu.with_memory_space_constraint(down_weight[0], pltpu.HBM)
    core = lax.axis_index("core").astype(jnp.int32).reshape(1)

    def swap_cores(value):
        return lax.ppermute(value, "core", [(0, 1), (1, 0)])

    def exchange(value):
        return lax.all_to_all(value, ("xhi", "expert"), split_axis=0, concat_axis=0, tiled=True)

    def select(hit, value):
        picks = jnp.broadcast_to(
            hit[None, :, None], (n_xhi, EXPERTS, per_expert, CAPACITY, rows)
        ).reshape(peers * CAPACITY, rows)
        sent = jnp.dot(
            picks.astype(jnp.bfloat16), value, preferred_element_type=jnp.float32
        ).astype(jnp.bfloat16)
        return sent.reshape(peers, CAPACITY, quarter)

    def deliver(sent):
        return exchange(sent).reshape(n_xhi, n_expert * CAPACITY, quarter)

    def combine(current, mixing, arrived):
        summed = jnp.sum(
            arrived.reshape(n_xhi, EXPERTS, per_expert, CAPACITY, quarter).astype(jnp.float32),
            axis=(0, 2),
        )
        moe_term = lax.dot_general(
            mixing,
            summed.reshape(EXPERTS * CAPACITY, quarter),
            (((0,), (0,)), ((), ())),
            precision=lax.Precision.HIGHEST,
            preferred_element_type=jnp.float32,
        )
        result = (current.astype(jnp.float32) + moe_term).astype(jnp.bfloat16)
        return lax.ppermute(
            result, "section", [(i, (i - 1) % n_section) for i in range(n_section)]
        )

    def outgoing(send, keep):
        return (
            keep.astype(jnp.float32) + swap_cores(send).astype(jnp.float32)
        ).astype(jnp.bfloat16).reshape(peers, CAPACITY, quarter)

    picked = []
    for step_index in range(plan.shape[1]):
        micro = plan[0, step_index]
        saved_now = lax.dynamic_index_in_dim(saved_input[0], micro, 0, keepdims=False)
        route_now = lax.dynamic_index_in_dim(routes[0], micro, 0, keepdims=False)
        share_now = lax.dynamic_index_in_dim(route_weights[0], micro, 0, keepdims=False)
        hit, mixing = slots(route_now, share_now)
        picked.append((hit, mixing, select(hit, saved_now)))

    ticks = len(picked)
    current = grad_in[0]
    saved_rows = deliver(picked[0][2])
    for tick in range(ticks):
        hit, mixing, _ = picked[tick]
        grad_sent, saved_rows = together(select(hit, current), saved_rows)
        grad_rows = deliver(grad_sent)
        factors = pltpu.with_memory_space_constraint(
            factor(core, saved_rows, swap_cores(saved_rows), up_local), pltpu.HBM
        )
        grad_rows, factors = together(grad_rows, factors)
        if tick + 1 < ticks:
            saved_sent, grad_rows = together(picked[tick + 1][2], grad_rows)
            saved_rows = deliver(saved_sent)
        send, keep = branch(core, grad_rows, swap_cores(grad_rows), down_local, factors, up_local)
        if tick + 1 < ticks:
            send, saved_rows = together(send, saved_rows)
        current = combine(current, mixing, exchange(outgoing(send, keep)))
    return current[None]


def solution(mesh):
    sections, experts, parts = (mesh.shape[name] for name in ("section", "expert", "mp"))
    refined = Mesh(
        mesh.devices.reshape(sections, experts, parts // 2, 2),
        ("section", "expert", "xhi", "core"),
    )
    mp = ("xhi", "core")
    placed = (
        P("section", "expert", mp),
        P("section", None, "expert", mp),
        P("section", None, "expert", None),
        P("section", None, "expert", None),
        P("section", None),
        P("section", None, ("expert", "xhi", "core")),
        P("section", ("expert", "xhi", "core"), None),
    )
    return jax.shard_map(
        per_device,
        mesh=refined,
        in_specs=placed,
        out_specs=P("section", "expert", mp),
        check_vma=False,
    )
```

```python
import jax
import jax.numpy as jnp
from jax import lax
from jax.experimental import pallas as pl
from jax.experimental.pallas import tpu as pltpu
from jax.sharding import Mesh, PartitionSpec as P

EXPERTS = 4
CAPACITY = 72
HIDDEN_BLOCK = 256
VMEM_LIMIT = 32 * 1024 * 1024


def together(*values):
    return lax.optimization_barrier(values)


def contract_last(left, right):
    return lax.dot_general(
        left, right, (((1,), (1,)), ((), ())), preferred_element_type=jnp.float32
    )


def factor_kernel(core_ref, mine_ref, other_ref, up_ref, factor_ref):
    core = core_ref[0]
    quarter = mine_ref.shape[2]
    pre = None
    for xhi in range(mine_ref.shape[0]):
        own = pl.multiple_of((2 * xhi + core) * quarter, quarter)
        theirs = pl.multiple_of((2 * xhi + 1 - core) * quarter, quarter)
        part = jnp.dot(
            mine_ref[xhi], up_ref[pl.ds(own, quarter), :], preferred_element_type=jnp.float32
        ) + jnp.dot(
            other_ref[xhi], up_ref[pl.ds(theirs, quarter), :], preferred_element_type=jnp.float32
        )
        pre = part if pre is None else pre + part
    sigma = jax.nn.sigmoid(pre)
    factor_ref[...] = sigma * (1.0 + pre * (1.0 - sigma))


def factor(core, saved, up):
    mine, other, column = saved
    halves, rows = mine.shape[:2]
    width, hidden = up.shape
    quarter = width // (2 * halves)
    whole = pl.BlockSpec((halves, rows, quarter), lambda i, c: (0, 0, column))
    return pl.pallas_call(
        factor_kernel,
        out_shape=pltpu.HBM((rows, hidden), jnp.float32),
        grid_spec=pltpu.PrefetchScalarGridSpec(
            num_scalar_prefetch=1,
            grid=(hidden // HIDDEN_BLOCK,),
            in_specs=[whole, whole, pl.BlockSpec((width, HIDDEN_BLOCK), lambda i, c: (0, i))],
            out_specs=pl.BlockSpec((rows, HIDDEN_BLOCK), lambda i, c: (0, i)),
        ),
        compiler_params=pltpu.CompilerParams(
            dimension_semantics=("arbitrary",), vmem_limit_bytes=VMEM_LIMIT
        ),
        cost_estimate=pl.CostEstimate(
            flops=2 * rows * width * hidden,
            transcendentals=2 * rows * hidden,
            bytes_accessed=2 * width * (rows + hidden) + 4 * rows * hidden,
        ),
        name="factor",
    )(core, mine, other, up)


def sent_kernel(
    core_ref, mine_ref, other_ref, down_ref, factor_ref, up_ref, grad_pre_ref, send_ref
):
    core = core_ref[0]
    step = pl.program_id(0)
    halves, _, quarter = mine_ref.shape
    blocks = grad_pre_ref.shape[1] // HIDDEN_BLOCK

    for block in range(blocks):

        @pl.when(step == block)
        def _(block=block):
            act = None
            for xhi in range(halves):
                own = pl.multiple_of((2 * xhi + core) * quarter, quarter)
                theirs = pl.multiple_of((2 * xhi + 1 - core) * quarter, quarter)
                part = contract_last(
                    mine_ref[xhi], down_ref[:, pl.ds(own, quarter)]
                ) + contract_last(other_ref[xhi], down_ref[:, pl.ds(theirs, quarter)])
                act = part if act is None else act + part
            grad_pre_ref[:, block * HIDDEN_BLOCK : (block + 1) * HIDDEN_BLOCK] = (
                act * factor_ref[...]
            ).astype(jnp.bfloat16)

    @pl.when(step >= blocks)
    def _():
        send_ref[0] = contract_last(grad_pre_ref[...], up_ref[...]).astype(jnp.bfloat16)


def sent_part(core, grads, down, factors, up):
    mine, other, column = grads
    halves, rows = mine.shape[:2]
    hidden, width = down.shape
    quarter = width // (2 * halves)
    blocks = hidden // HIDDEN_BLOCK
    whole = pl.BlockSpec((halves, rows, quarter), lambda i, c: (0, 0, column))

    def hidden_block(i):
        return jnp.minimum(i, blocks - 1)

    def late(i):
        return jnp.maximum(i - blocks, 0)

    return pl.pallas_call(
        sent_kernel,
        out_shape=(
            jax.ShapeDtypeStruct((rows, hidden), jnp.bfloat16),
            jax.ShapeDtypeStruct((halves, rows, quarter), jnp.bfloat16),
        ),
        grid_spec=pltpu.PrefetchScalarGridSpec(
            num_scalar_prefetch=1,
            grid=(blocks + halves,),
            in_specs=[
                whole,
                whole,
                pl.BlockSpec((HIDDEN_BLOCK, width), lambda i, c: (hidden_block(i), 0)),
                pl.BlockSpec((rows, HIDDEN_BLOCK), lambda i, c: (0, hidden_block(i))),
                pl.BlockSpec((quarter, hidden), lambda i, c: (2 * late(i) + 1 - c[0], 0)),
            ],
            out_specs=(
                pl.BlockSpec((rows, hidden), lambda i, c: (0, 0)),
                pl.BlockSpec((1, rows, quarter), lambda i, c: (late(i), 0, 0)),
            ),
        ),
        compiler_params=pltpu.CompilerParams(
            dimension_semantics=("arbitrary",), vmem_limit_bytes=VMEM_LIMIT
        ),
        cost_estimate=pl.CostEstimate(
            flops=4 * rows * hidden, transcendentals=0, bytes_accessed=4 * rows * hidden
        ),
        name="sent_part",
    )(core, mine, other, down, factors, up)


def kept_kernel(core_ref, grad_pre_ref, up_ref, keep_ref):
    keep_ref[0] = contract_last(grad_pre_ref[...], up_ref[...]).astype(jnp.bfloat16)


def kept_part(core, grad_pre, up):
    rows, hidden = grad_pre.shape
    quarter = up.shape[0] // 4
    halves = 2
    return pl.pallas_call(
        kept_kernel,
        out_shape=jax.ShapeDtypeStruct((halves, rows, quarter), jnp.bfloat16),
        grid_spec=pltpu.PrefetchScalarGridSpec(
            num_scalar_prefetch=1,
            grid=(halves,),
            in_specs=[
                pl.BlockSpec((rows, hidden), lambda i, c: (0, 0)),
                pl.BlockSpec((quarter, hidden), lambda i, c: (2 * i + c[0], 0)),
            ],
            out_specs=pl.BlockSpec((1, rows, quarter), lambda i, c: (i, 0, 0)),
        ),
        compiler_params=pltpu.CompilerParams(
            dimension_semantics=("arbitrary",), vmem_limit_bytes=VMEM_LIMIT
        ),
        cost_estimate=pl.CostEstimate(
            flops=2 * rows * hidden * halves * quarter,
            transcendentals=0,
            bytes_accessed=2 * hidden * (rows + halves * quarter),
        ),
        name="kept_part",
    )(core, grad_pre, up)


def pick_kernel(step, plan_ref, routes_ref, *refs):
    del plan_ref
    values, out_ref = refs[:-1], refs[-1]
    expert = pl.program_id(0)
    rows = routes_ref.shape[2]
    named = (routes_ref[0] == expert).astype(jnp.float32)
    chosen = jnp.max(named, axis=0, keepdims=True)
    earlier = (
        lax.broadcasted_iota(jnp.int32, (rows, rows), 0)
        < lax.broadcasted_iota(jnp.int32, (rows, rows), 1)
    ).astype(jnp.bfloat16)
    before = jnp.dot(
        jnp.broadcast_to(chosen, (16, rows)).astype(jnp.bfloat16),
        earlier,
        preferred_element_type=jnp.float32,
    )[0:1]
    place = jnp.where(chosen > 0.0, before, -1.0).astype(jnp.int32)
    hit = place == lax.broadcasted_iota(jnp.int32, (CAPACITY, rows), 0)
    select = hit.astype(jnp.float32).astype(jnp.bfloat16)
    copies = [(i, k) for i in range(out_ref.shape[0]) for k in range(out_ref.shape[2])]
    start = 0
    for value_ref in values:
        value = value_ref[0]
        width = value.shape[1]
        rows_sent = jnp.dot(select, value, preferred_element_type=jnp.float32).astype(jnp.bfloat16)
        for i, k in copies:
            out_ref[i, 0, k, :, start : start + width] = rows_sent
        start += width


def pick(step, plan, routes, values, n_xhi, per_expert):
    rows = routes.shape[2]
    width = sum(value.shape[2] for value, _ in values)
    specs = [pl.BlockSpec((1,) + routes.shape[1:], lambda j, p: (p[step], 0, 0))]
    for value, planned in values:
        if planned:
            specs.append(pl.BlockSpec((1,) + value.shape[1:], lambda j, p: (p[step], 0, 0)))
        else:
            specs.append(pl.BlockSpec((1,) + value.shape[1:], lambda j, p: (0, 0, 0)))
    out = pl.pallas_call(
        lambda *refs: pick_kernel(step, *refs),
        out_shape=jax.ShapeDtypeStruct(
            (n_xhi, EXPERTS, per_expert, CAPACITY, width), jnp.bfloat16
        ),
        grid_spec=pltpu.PrefetchScalarGridSpec(
            num_scalar_prefetch=1,
            grid=(EXPERTS,),
            in_specs=specs,
            out_specs=pl.BlockSpec(
                (n_xhi, 1, per_expert, CAPACITY, width), lambda j, p: (0, j, 0, 0, 0)
            ),
        ),
        compiler_params=pltpu.CompilerParams(dimension_semantics=("arbitrary",)),
        name="pick",
    )(plan, routes, *[value for value, _ in values])
    return out.reshape(n_xhi * EXPERTS * per_expert, CAPACITY, width)


def slots(route_now, share_now):
    rows = route_now.shape[0]
    named = route_now.T[None] == jnp.arange(EXPERTS, dtype=jnp.int32)[:, None, None]
    chosen = jnp.any(named, axis=1)
    mix = jnp.sum(jnp.where(named, share_now.T[None], 0.0), axis=1)
    token = jnp.arange(rows, dtype=jnp.int32)
    earlier = (token[:, None] < token[None, :]).astype(jnp.bfloat16)
    before = jnp.dot(
        chosen.astype(jnp.bfloat16), earlier, preferred_element_type=jnp.float32
    ).astype(jnp.int32)
    place = jnp.where(chosen, before, -1)
    hit = place[:, None, :] == jnp.arange(CAPACITY, dtype=jnp.int32)[None, :, None]
    mixing = jnp.where(hit, mix[:, None, :], 0.0).reshape(EXPERTS * CAPACITY, rows)
    return mixing


def per_device(grad_in, saved_input, routes, route_weights, plan, up_weight, down_weight):
    n_expert = lax.axis_size("expert")
    n_xhi = lax.axis_size("xhi")
    n_section = lax.axis_size("section")
    per_expert = n_expert // EXPERTS
    peers = n_xhi * n_expert
    rows, quarter = grad_in.shape[1:]
    up_local = pltpu.with_memory_space_constraint(up_weight[0], pltpu.HBM)
    down_local = pltpu.with_memory_space_constraint(down_weight[0], pltpu.HBM)
    core = lax.axis_index("core").astype(jnp.int32).reshape(1)

    def swap_cores(value):
        return lax.ppermute(value, "core", [(0, 1), (1, 0)])

    def exchange(value):
        return lax.all_to_all(value, ("xhi", "expert"), split_axis=0, concat_axis=0, tiled=True)

    def deliver(sent):
        return exchange(sent).reshape(n_xhi, n_expert * CAPACITY, sent.shape[2])

    def combine(current, mixing, arrived):
        summed = jnp.sum(
            arrived.reshape(n_xhi, EXPERTS, per_expert, CAPACITY, quarter).astype(jnp.float32),
            axis=(0, 2),
        )
        moe_term = lax.dot_general(
            mixing,
            summed.reshape(EXPERTS * CAPACITY, quarter),
            (((0,), (0,)), ((), ())),
            precision=lax.Precision.HIGHEST,
            preferred_element_type=jnp.float32,
        )
        result = (current.astype(jnp.float32) + moe_term).astype(jnp.bfloat16)
        return lax.ppermute(
            result, "section", [(i, (i - 1) % n_section) for i in range(n_section)]
        )

    def outgoing(send, keep):
        return (
            keep.astype(jnp.float32) + swap_cores(send).astype(jnp.float32)
        ).astype(jnp.bfloat16).reshape(peers, CAPACITY, quarter)

    micros = plan[0]
    routes_by_choice = routes[0].transpose(0, 2, 1)
    saved_all = saved_input[0]
    current = grad_in[0]
    ticks = micros.shape[0]

    def mixing_of(tick):
        route_now = lax.dynamic_index_in_dim(routes[0], micros[tick], 0, keepdims=False)
        share_now = lax.dynamic_index_in_dim(route_weights[0], micros[tick], 0, keepdims=False)
        return slots(route_now, share_now)

    def pick_rows(tick, *values):
        return pick(tick, micros, routes_by_choice, values, n_xhi, per_expert)

    def in_hbm(value):
        return pltpu.with_memory_space_constraint(value, pltpu.HBM)

    rows_in = deliver(pick_rows(0, (saved_all, True), (current[None], False)))
    later = None
    for tick in range(ticks):
        if tick == 0:
            both, swapped = rows_in, None
            if ticks > 1:
                saved_sent, both = together(pick_rows(1, (saved_all, True)), both)
                later = deliver(saved_sent)
            swapped = swap_cores(both)
            saved, grads = (both, swapped, 0), (both, swapped, 1)
            factors = in_hbm(factor(core, saved, up_local))
        else:
            grad_sent, later = together(pick_rows(tick, (current[None], False)), later)
            grad_rows = deliver(grad_sent)
            factors = in_hbm(factor(core, (later, swap_cores(later), 0), up_local))
            grad_rows, factors = together(grad_rows, factors)
            grads = (grad_rows, swap_cores(grad_rows), 0)
        grad_pre, send = sent_part(core, grads, down_local, factors, up_local)
        keep = kept_part(core, grad_pre, up_local)
        if tick + 1 < ticks:
            send, later, keep = together(send, later, keep)
        partial_rows = (
            keep.astype(jnp.float32) + swap_cores(send).astype(jnp.float32)
        ).astype(jnp.bfloat16)
        arrived = exchange(partial_rows.reshape(peers, CAPACITY, quarter))
        current = combine(current, mixing_of(tick), arrived)
    return current[None]


def solution(mesh):
    sections, experts, parts = (mesh.shape[name] for name in ("section", "expert", "mp"))
    refined = Mesh(
        mesh.devices.reshape(sections, experts, parts // 2, 2),
        ("section", "expert", "xhi", "core"),
    )
    mp = ("xhi", "core")
    placed = (
        P("section", "expert", mp),
        P("section", None, "expert", mp),
        P("section", None, "expert", None),
        P("section", None, "expert", None),
        P("section", None),
        P("section", None, ("expert", "xhi", "core")),
        P("section", ("expert", "xhi", "core"), None),
    )
    return jax.shard_map(
        per_device,
        mesh=refined,
        in_specs=placed,
        out_specs=P("section", "expert", mp),
        check_vma=False,
    )
```

```python
import jax
import jax.numpy as jnp
from jax import lax
from jax.experimental import pallas as pl
from jax.experimental.pallas import tpu as pltpu
from jax.sharding import Mesh, PartitionSpec as P

EXPERTS = 4
CAPACITY = 72
HIDDEN_BLOCK = 256
VMEM_LIMIT = 32 * 1024 * 1024


def together(*values):
    return lax.optimization_barrier(values)


def contract_last(left, right):
    return lax.dot_general(
        left, right, (((1,), (1,)), ((), ())), preferred_element_type=jnp.float32
    )


def quarter_copies(core, mine, other, column, weight, by_rows, rows_buf, weight_buf, semaphores):
    quarter = rows_buf.shape[2]
    copies = []
    for number in range(rows_buf.shape[0]):
        xhi = number % mine.shape[0]
        swapped = number // mine.shape[0]
        first = pl.multiple_of((2 * xhi + (1 - core if swapped else core)) * quarter, quarter)
        part = pl.ds(first, quarter)
        source = other if swapped else mine
        copies.append(
            (
                pltpu.make_async_copy(
                    source.at[xhi, :, pl.ds(column * quarter, quarter)],
                    rows_buf.at[number],
                    semaphores.at[2 * number],
                ),
                pltpu.make_async_copy(
                    weight.at[part, :] if by_rows else weight.at[:, part],
                    weight_buf.at[number],
                    semaphores.at[2 * number + 1],
                ),
            )
        )
    return copies


def hidden_blocks(hidden):
    return [slice(start, start + HIDDEN_BLOCK) for start in range(0, hidden, HIDDEN_BLOCK)]


def factor_kernel(
    column, core_ref, mine, other, up, out, rows_buf, up_buf, acc, semaphores, out_semaphores
):
    copies = quarter_copies(
        core_ref[0], mine, other, column, up, True, rows_buf, up_buf, semaphores
    )
    for pair in copies:
        for copy in pair:
            copy.start()
    last = len(copies) - 1
    blocks = hidden_blocks(acc.shape[1])
    sent = []
    for number, pair in enumerate(copies):
        for copy in pair:
            copy.wait()
        for index, block in enumerate(blocks):
            part = jnp.dot(
                rows_buf[number], up_buf[number, :, block], preferred_element_type=jnp.float32
            )
            if number:
                part = acc[:, block] + part
            if number < last:
                acc[:, block] = part
                continue
            sigma = jax.nn.sigmoid(part)
            acc[:, block] = sigma * (1.0 + part * (1.0 - sigma))
            sent.append(
                pltpu.make_async_copy(
                    acc.at[:, block], out.at[:, block], out_semaphores.at[index]
                )
            )
            sent[-1].start()
    for copy in sent:
        copy.wait()


def own_copies(kernel, name, out, scratch, core, *operands):
    anywhere = pl.BlockSpec(memory_space=pltpu.HBM)
    return pl.pallas_call(
        kernel,
        out_shape=out,
        in_specs=[pl.BlockSpec(memory_space=pltpu.SMEM)] + [anywhere] * len(operands),
        out_specs=jax.tree.map(lambda _: anywhere, out),
        scratch_shapes=scratch,
        compiler_params=pltpu.CompilerParams(vmem_limit_bytes=VMEM_LIMIT),
        cost_estimate=pl.CostEstimate(flops=1000, transcendentals=0, bytes_accessed=1000),
        name=name,
    )(core, *operands)


def factor(core, saved, up):
    mine, other, column = saved
    halves, rows = mine.shape[:2]
    width, hidden = up.shape
    pieces = 2 * halves
    quarter = width // pieces
    return own_copies(
        lambda *refs: factor_kernel(column, *refs),
        "factor",
        jax.ShapeDtypeStruct((rows, hidden), jnp.float32),
        [
            pltpu.VMEM((pieces, rows, quarter), jnp.bfloat16),
            pltpu.VMEM((pieces, quarter, hidden), jnp.bfloat16),
            pltpu.VMEM((rows, hidden), jnp.float32),
            pltpu.SemaphoreType.DMA((2 * pieces,)),
            pltpu.SemaphoreType.DMA((hidden // HIDDEN_BLOCK,)),
        ],
        core,
        mine,
        other,
        up,
    )


def sent_kernel(
    column,
    core_ref,
    mine,
    other,
    down,
    factors,
    up,
    grad_pre_out,
    send_out,
    rows_buf,
    down_buf,
    acc,
    factor_buf,
    up_buf,
    grad_pre,
    send,
    semaphores,
    late_semaphores,
):
    core = core_ref[0]
    halves, _, quarter = send.shape
    copies = quarter_copies(
        core, mine, other, column, down, False, rows_buf, down_buf, semaphores
    )
    factor_copy = pltpu.make_async_copy(factors, factor_buf, late_semaphores.at[0])
    up_copies = [
        pltpu.make_async_copy(
            up.at[pl.ds(pl.multiple_of((2 * half + 1 - core) * quarter, quarter), quarter), :],
            up_buf.at[half],
            late_semaphores.at[1 + half],
        )
        for half in range(halves)
    ]
    for pair in copies:
        for copy in pair:
            copy.start()
    factor_copy.start()
    for copy in up_copies:
        copy.start()
    last = len(copies) - 1
    blocks = hidden_blocks(acc.shape[1])
    for number, pair in enumerate(copies):
        for copy in pair:
            copy.wait()
        if number == last:
            factor_copy.wait()
        for block in blocks:
            part = contract_last(rows_buf[number], down_buf[number, block, :])
            if number:
                part = acc[:, block] + part
            if number < last:
                acc[:, block] = part
            else:
                grad_pre[:, block] = (part * factor_buf[:, block]).astype(jnp.bfloat16)
    sent = [pltpu.make_async_copy(grad_pre, grad_pre_out, late_semaphores.at[1 + halves])]
    sent[0].start()
    for half in range(halves):
        up_copies[half].wait()
        send[half] = contract_last(grad_pre[...], up_buf[half]).astype(jnp.bfloat16)
        sent.append(
            pltpu.make_async_copy(
                send.at[half], send_out.at[half], late_semaphores.at[2 + halves + half]
            )
        )
        sent[-1].start()
    for copy in sent:
        copy.wait()


def sent_part(core, grads, down, factors, up):
    mine, other, column = grads
    halves, rows = mine.shape[:2]
    hidden, width = down.shape
    pieces = 2 * halves
    quarter = width // pieces
    return own_copies(
        lambda *refs: sent_kernel(column, *refs),
        "sent_part",
        (
            jax.ShapeDtypeStruct((rows, hidden), jnp.bfloat16),
            jax.ShapeDtypeStruct((halves, rows, quarter), jnp.bfloat16),
        ),
        [
            pltpu.VMEM((pieces, rows, quarter), jnp.bfloat16),
            pltpu.VMEM((pieces, hidden, quarter), jnp.bfloat16),
            pltpu.VMEM((rows, hidden), jnp.float32),
            pltpu.VMEM((rows, hidden), jnp.float32),
            pltpu.VMEM((halves, quarter, hidden), jnp.bfloat16),
            pltpu.VMEM((rows, hidden), jnp.bfloat16),
            pltpu.VMEM((halves, rows, quarter), jnp.bfloat16),
            pltpu.SemaphoreType.DMA((2 * pieces,)),
            pltpu.SemaphoreType.DMA((2 + 2 * halves,)),
        ],
        core,
        mine,
        other,
        down,
        factors,
        up,
    )


def kept_kernel(core_ref, grad_pre_ref, up_ref, keep_ref):
    keep_ref[0] = contract_last(grad_pre_ref[...], up_ref[...]).astype(jnp.bfloat16)


def kept_part(core, grad_pre, up):
    rows, hidden = grad_pre.shape
    quarter = up.shape[0] // 4
    halves = 2
    return pl.pallas_call(
        kept_kernel,
        out_shape=jax.ShapeDtypeStruct((halves, rows, quarter), jnp.bfloat16),
        grid_spec=pltpu.PrefetchScalarGridSpec(
            num_scalar_prefetch=1,
            grid=(halves,),
            in_specs=[
                pl.BlockSpec((rows, hidden), lambda i, c: (0, 0)),
                pl.BlockSpec((quarter, hidden), lambda i, c: (2 * i + c[0], 0)),
            ],
            out_specs=pl.BlockSpec((1, rows, quarter), lambda i, c: (i, 0, 0)),
        ),
        compiler_params=pltpu.CompilerParams(
            dimension_semantics=("arbitrary",), vmem_limit_bytes=VMEM_LIMIT
        ),
        cost_estimate=pl.CostEstimate(
            flops=2 * rows * hidden * halves * quarter,
            transcendentals=0,
            bytes_accessed=2 * hidden * (rows + halves * quarter),
        ),
        name="kept_part",
    )(core, grad_pre, up)


def pick_kernel(plan_ref, routes_ref, *refs):
    del plan_ref
    values, (out, buffer, semaphores) = refs[:-3], refs[-3:]
    rows = routes_ref.shape[2]
    expert = lax.broadcasted_iota(jnp.int32, (16, rows), 0)
    named = routes_ref[0]
    chosen = named[0:1] == expert
    for choice in range(1, named.shape[0]):
        chosen = chosen | (named[choice : choice + 1] == expert)
    earlier = (
        lax.broadcasted_iota(jnp.int32, (rows, rows), 0)
        < lax.broadcasted_iota(jnp.int32, (rows, rows), 1)
    ).astype(jnp.float32)
    before = jnp.dot(
        chosen.astype(jnp.float32).astype(jnp.bfloat16),
        earlier.astype(jnp.bfloat16),
        preferred_element_type=jnp.float32,
    )
    place = jnp.where(chosen, before, -1.0).astype(jnp.int32)
    slot = lax.broadcasted_iota(jnp.int32, (CAPACITY, rows), 0)
    copies = []
    for j in range(EXPERTS):
        select = (place[j : j + 1] == slot).astype(jnp.float32).astype(jnp.bfloat16)
        start = 0
        for value_ref in values:
            width = value_ref.shape[2]
            buffer[j, :, start : start + width] = jnp.dot(
                select, value_ref[0], preferred_element_type=jnp.float32
            ).astype(jnp.bfloat16)
            start += width
        for i in range(out.shape[0]):
            for k in range(out.shape[2]):
                copy = pltpu.make_async_copy(
                    buffer.at[j], out.at[i, j, k], semaphores.at[len(copies)]
                )
                copy.start()
                copies.append(copy)
    for copy in copies:
        copy.wait()


def pick(step, plan, routes, values, n_xhi, per_expert):
    width = sum(value.shape[2] for value, _ in values)
    specs = [pl.BlockSpec((1,) + routes.shape[1:], lambda i, p: (p[step], 0, 0))]
    for value, planned in values:
        if planned:
            specs.append(pl.BlockSpec((1,) + value.shape[1:], lambda i, p: (p[step], 0, 0)))
        else:
            specs.append(pl.BlockSpec((1,) + value.shape[1:], lambda i, p: (0, 0, 0)))
    out = pl.pallas_call(
        pick_kernel,
        out_shape=jax.ShapeDtypeStruct(
            (n_xhi, EXPERTS, per_expert, CAPACITY, width), jnp.bfloat16
        ),
        grid_spec=pltpu.PrefetchScalarGridSpec(
            num_scalar_prefetch=1,
            grid=(1,),
            in_specs=specs,
            out_specs=pl.BlockSpec(memory_space=pltpu.HBM),
            scratch_shapes=[
                pltpu.VMEM((EXPERTS, CAPACITY, width), jnp.bfloat16),
                pltpu.SemaphoreType.DMA((n_xhi * EXPERTS * per_expert,)),
            ],
        ),
        compiler_params=pltpu.CompilerParams(dimension_semantics=("arbitrary",)),
        name="pick",
    )(plan, routes, *[value for value, _ in values])
    return out.reshape(n_xhi * EXPERTS * per_expert, CAPACITY, width)


def slots(route_now, share_now):
    rows = route_now.shape[0]
    named = route_now.T[None] == jnp.arange(EXPERTS, dtype=jnp.int32)[:, None, None]
    chosen = jnp.any(named, axis=1)
    mix = jnp.sum(jnp.where(named, share_now.T[None], 0.0), axis=1)
    token = jnp.arange(rows, dtype=jnp.int32)
    earlier = (token[:, None] < token[None, :]).astype(jnp.bfloat16)
    before = jnp.dot(
        chosen.astype(jnp.bfloat16), earlier, preferred_element_type=jnp.float32
    ).astype(jnp.int32)
    place = jnp.where(chosen, before, -1)
    hit = place[:, None, :] == jnp.arange(CAPACITY, dtype=jnp.int32)[None, :, None]
    mixing = jnp.where(hit, mix[:, None, :], 0.0).reshape(EXPERTS * CAPACITY, rows)
    return mixing


def per_device(grad_in, saved_input, routes, route_weights, plan, up_weight, down_weight):
    n_expert = lax.axis_size("expert")
    n_xhi = lax.axis_size("xhi")
    n_section = lax.axis_size("section")
    per_expert = n_expert // EXPERTS
    peers = n_xhi * n_expert
    rows, quarter = grad_in.shape[1:]
    up_local = pltpu.with_memory_space_constraint(up_weight[0], pltpu.HBM)
    down_local = pltpu.with_memory_space_constraint(down_weight[0], pltpu.HBM)
    core = lax.axis_index("core").astype(jnp.int32).reshape(1)

    def swap_cores(value):
        return lax.ppermute(value, "core", [(0, 1), (1, 0)])

    def exchange(value):
        return lax.all_to_all(value, ("xhi", "expert"), split_axis=0, concat_axis=0, tiled=True)

    def deliver(sent):
        return exchange(sent).reshape(n_xhi, n_expert * CAPACITY, sent.shape[2])

    def combine(current, mixing, arrived):
        summed = jnp.sum(
            arrived.reshape(n_xhi, EXPERTS, per_expert, CAPACITY, quarter).astype(jnp.float32),
            axis=(0, 2),
        )
        moe_term = lax.dot_general(
            mixing,
            summed.reshape(EXPERTS * CAPACITY, quarter),
            (((0,), (0,)), ((), ())),
            precision=lax.Precision.HIGHEST,
            preferred_element_type=jnp.float32,
        )
        result = (current.astype(jnp.float32) + moe_term).astype(jnp.bfloat16)
        return lax.ppermute(
            result, "section", [(i, (i - 1) % n_section) for i in range(n_section)]
        )

    def outgoing(send, keep):
        return (
            keep.astype(jnp.float32) + swap_cores(send).astype(jnp.float32)
        ).astype(jnp.bfloat16).reshape(peers, CAPACITY, quarter)

    micros = plan[0]
    routes_by_choice = routes[0].transpose(0, 2, 1)
    saved_all = saved_input[0]
    current = grad_in[0]
    ticks = micros.shape[0]

    def mixing_of(tick):
        route_now = lax.dynamic_index_in_dim(routes[0], micros[tick], 0, keepdims=False)
        share_now = lax.dynamic_index_in_dim(route_weights[0], micros[tick], 0, keepdims=False)
        return slots(route_now, share_now)

    def pick_rows(tick, *values):
        return pick(tick, micros, routes_by_choice, values, n_xhi, per_expert)

    rows_in = deliver(pick_rows(0, (saved_all, True), (current[None], False)))
    later = None
    for tick in range(ticks):
        if tick == 0:
            both, swapped = rows_in, None
            if ticks > 1:
                saved_sent, both = together(pick_rows(1, (saved_all, True)), both)
                later = deliver(saved_sent)
            swapped = swap_cores(both)
            saved, grads = (both, swapped, 0), (both, swapped, 1)
            factors = factor(core, saved, up_local)
        else:
            grad_sent, later = together(pick_rows(tick, (current[None], False)), later)
            grad_rows = deliver(grad_sent)
            factors = factor(core, (later, swap_cores(later), 0), up_local)
            grad_rows, factors = together(grad_rows, factors)
            grads = (grad_rows, swap_cores(grad_rows), 0)
        grad_pre, send = sent_part(core, grads, down_local, factors, up_local)
        keep = kept_part(core, grad_pre, up_local)
        if tick + 1 < ticks:
            send, later, keep = together(send, later, keep)
        partial_rows = (
            keep.astype(jnp.float32) + swap_cores(send).astype(jnp.float32)
        ).astype(jnp.bfloat16)
        arrived = exchange(partial_rows.reshape(peers, CAPACITY, quarter))
        current = combine(current, mixing_of(tick), arrived)
    return current[None]


def solution(mesh):
    sections, experts, parts = (mesh.shape[name] for name in ("section", "expert", "mp"))
    refined = Mesh(
        mesh.devices.reshape(sections, experts, parts // 2, 2),
        ("section", "expert", "xhi", "core"),
    )
    mp = ("xhi", "core")
    placed = (
        P("section", "expert", mp),
        P("section", None, "expert", mp),
        P("section", None, "expert", None),
        P("section", None, "expert", None),
        P("section", None),
        P("section", None, ("expert", "xhi", "core")),
        P("section", ("expert", "xhi", "core"), None),
    )
    return jax.shard_map(
        per_device,
        mesh=refined,
        in_specs=placed,
        out_specs=P("section", "expert", mp),
        check_vma=False,
    )
```

```python
import jax
import jax.numpy as jnp
from jax import lax
from jax.experimental import pallas as pl
from jax.experimental.pallas import tpu as pltpu
from jax.sharding import Mesh, PartitionSpec as P

EXPERTS = 4
CAPACITY = 72
HIDDEN_BLOCK = 256
VMEM_LIMIT = 32 * 1024 * 1024


def together(*values):
    return lax.optimization_barrier(values)


def contract_last(left, right):
    return lax.dot_general(
        left, right, (((1,), (1,)), ((), ())), preferred_element_type=jnp.float32
    )


def quarter_copies(core, mine, other, column, weight, by_rows, rows_buf, weight_buf, semaphores):
    quarter = rows_buf.shape[2]
    copies = []
    for number in range(rows_buf.shape[0]):
        xhi = number % mine.shape[0]
        swapped = number // mine.shape[0]
        first = pl.multiple_of((2 * xhi + (1 - core if swapped else core)) * quarter, quarter)
        part = pl.ds(first, quarter)
        source = other if swapped else mine
        copies.append(
            (
                pltpu.make_async_copy(
                    source.at[xhi, :, pl.ds(column * quarter, quarter)],
                    rows_buf.at[number],
                    semaphores.at[2 * number],
                ),
                pltpu.make_async_copy(
                    weight.at[part, :] if by_rows else weight.at[:, part],
                    weight_buf.at[number],
                    semaphores.at[2 * number + 1],
                ),
            )
        )
    return copies


def hidden_blocks(hidden):
    return [slice(start, start + HIDDEN_BLOCK) for start in range(0, hidden, HIDDEN_BLOCK)]


def factor_kernel(
    column, core_ref, mine, other, up, out, rows_buf, up_buf, acc, semaphores, out_semaphores
):
    copies = quarter_copies(
        core_ref[0], mine, other, column, up, True, rows_buf, up_buf, semaphores
    )
    for pair in copies:
        for copy in pair:
            copy.start()
    last = len(copies) - 1
    blocks = hidden_blocks(acc.shape[1])
    sent = []
    for number, pair in enumerate(copies):
        for copy in pair:
            copy.wait()
        for index, block in enumerate(blocks):
            part = jnp.dot(
                rows_buf[number], up_buf[number, :, block], preferred_element_type=jnp.float32
            )
            if number:
                part = acc[:, block] + part
            if number < last:
                acc[:, block] = part
                continue
            sigma = jax.nn.sigmoid(part)
            acc[:, block] = sigma * (1.0 + part * (1.0 - sigma))
            sent.append(
                pltpu.make_async_copy(
                    acc.at[:, block], out.at[:, block], out_semaphores.at[index]
                )
            )
            sent[-1].start()
    for copy in sent:
        copy.wait()


def own_copies(kernel, name, out, scratch, core, *operands):
    anywhere = pl.BlockSpec(memory_space=pltpu.HBM)
    return pl.pallas_call(
        kernel,
        out_shape=out,
        in_specs=[pl.BlockSpec(memory_space=pltpu.SMEM)] + [anywhere] * len(operands),
        out_specs=jax.tree.map(lambda _: anywhere, out),
        scratch_shapes=scratch,
        compiler_params=pltpu.CompilerParams(vmem_limit_bytes=VMEM_LIMIT),
        cost_estimate=pl.CostEstimate(flops=1000, transcendentals=0, bytes_accessed=1000),
        name=name,
    )(core, *operands)


def factor(core, saved, up):
    mine, other, column = saved
    halves, rows = mine.shape[:2]
    width, hidden = up.shape
    pieces = 2 * halves
    quarter = width // pieces
    return own_copies(
        lambda *refs: factor_kernel(column, *refs),
        "factor",
        jax.ShapeDtypeStruct((rows, hidden), jnp.float32),
        [
            pltpu.VMEM((pieces, rows, quarter), jnp.bfloat16),
            pltpu.VMEM((pieces, quarter, hidden), jnp.bfloat16),
            pltpu.VMEM((rows, hidden), jnp.float32),
            pltpu.SemaphoreType.DMA((2 * pieces,)),
            pltpu.SemaphoreType.DMA((hidden // HIDDEN_BLOCK,)),
        ],
        core,
        mine,
        other,
        up,
    )


def sent_kernel(
    column,
    complete,
    core_ref,
    mine,
    other,
    down,
    factors,
    up,
    first_out,
    second_out,
    rows_buf,
    down_buf,
    acc,
    factor_buf,
    up_buf,
    grad_pre,
    send,
    semaphores,
    late_semaphores,
):
    core = core_ref[0]
    halves = mine.shape[0]
    results, _, quarter = send.shape
    copies = quarter_copies(
        core, mine, other, column, down, False, rows_buf, down_buf, semaphores
    )
    firsts = [
        pl.multiple_of((2 * (n % halves) + (1 - core if n < halves else core)) * quarter, quarter)
        for n in range(results)
    ]
    factor_copy = pltpu.make_async_copy(factors, factor_buf, late_semaphores.at[0])
    up_copies = [
        pltpu.make_async_copy(
            up.at[pl.ds(firsts[n], quarter), :], up_buf.at[n], late_semaphores.at[1 + n]
        )
        for n in range(results)
    ]
    for pair in copies:
        for copy in pair:
            copy.start()
    factor_copy.start()
    for copy in up_copies:
        copy.start()
    last = len(copies) - 1
    blocks = hidden_blocks(acc.shape[1])
    for number, pair in enumerate(copies):
        for copy in pair:
            copy.wait()
        if number == last:
            factor_copy.wait()
        for block in blocks:
            part = contract_last(rows_buf[number], down_buf[number, block, :])
            if number:
                part = acc[:, block] + part
            if number < last:
                acc[:, block] = part
            else:
                grad_pre[:, block] = (part * factor_buf[:, block]).astype(jnp.bfloat16)
    sent = []
    if not complete:
        sent.append(
            pltpu.make_async_copy(grad_pre, first_out, late_semaphores.at[1 + 2 * results])
        )
        sent[-1].start()
    for n in range(results):
        up_copies[n].wait()
        send[n] = contract_last(grad_pre[...], up_buf[n]).astype(jnp.bfloat16)
        target = first_out if complete and n < halves else second_out
        sent.append(
            pltpu.make_async_copy(
                send.at[n], target.at[n % halves], late_semaphores.at[1 + results + n]
            )
        )
        sent[-1].start()
    for copy in sent:
        copy.wait()


def sent_part(core, grads, down, factors, up, complete):
    mine, other, column = grads
    halves, rows = mine.shape[:2]
    hidden, width = down.shape
    pieces = 2 * halves
    quarter = width // pieces
    results = pieces if complete else halves
    part = jax.ShapeDtypeStruct((halves, rows, quarter), jnp.bfloat16)
    if complete:
        kept = pltpu.HBM((halves, rows, quarter), jnp.bfloat16)
    else:
        kept = jax.ShapeDtypeStruct((rows, hidden), jnp.bfloat16)
    return own_copies(
        lambda *refs: sent_kernel(column, complete, *refs),
        "branch" if complete else "sent_part",
        (part, kept) if complete else (kept, part),
        [
            pltpu.VMEM((pieces, rows, quarter), jnp.bfloat16),
            pltpu.VMEM((pieces, hidden, quarter), jnp.bfloat16),
            pltpu.VMEM((rows, hidden), jnp.float32),
            pltpu.VMEM((rows, hidden), jnp.float32),
            pltpu.VMEM((results, quarter, hidden), jnp.bfloat16),
            pltpu.VMEM((rows, hidden), jnp.bfloat16),
            pltpu.VMEM((results, rows, quarter), jnp.bfloat16),
            pltpu.SemaphoreType.DMA((2 * pieces,)),
            pltpu.SemaphoreType.DMA((2 + 2 * results,)),
        ],
        core,
        mine,
        other,
        down,
        factors,
        up,
    )


def kept_kernel(core_ref, grad_pre_ref, up_ref, keep_ref):
    keep_ref[0] = contract_last(grad_pre_ref[...], up_ref[...]).astype(jnp.bfloat16)


def kept_part(core, grad_pre, up):
    rows, hidden = grad_pre.shape
    quarter = up.shape[0] // 4
    halves = 2
    return pl.pallas_call(
        kept_kernel,
        out_shape=jax.ShapeDtypeStruct((halves, rows, quarter), jnp.bfloat16),
        grid_spec=pltpu.PrefetchScalarGridSpec(
            num_scalar_prefetch=1,
            grid=(halves,),
            in_specs=[
                pl.BlockSpec((rows, hidden), lambda i, c: (0, 0)),
                pl.BlockSpec((quarter, hidden), lambda i, c: (2 * i + c[0], 0)),
            ],
            out_specs=pl.BlockSpec((1, rows, quarter), lambda i, c: (i, 0, 0)),
        ),
        compiler_params=pltpu.CompilerParams(
            dimension_semantics=("arbitrary",), vmem_limit_bytes=VMEM_LIMIT
        ),
        cost_estimate=pl.CostEstimate(
            flops=2 * rows * hidden * halves * quarter,
            transcendentals=0,
            bytes_accessed=2 * hidden * (rows + halves * quarter),
        ),
        name="kept_part",
    )(core, grad_pre, up)


def pick_kernel(plan_ref, routes_ref, *refs):
    del plan_ref
    values, (out, buffer, semaphores) = refs[:-3], refs[-3:]
    rows = routes_ref.shape[2]
    expert = lax.broadcasted_iota(jnp.int32, (16, rows), 0)
    named = routes_ref[0]
    chosen = named[0:1] == expert
    for choice in range(1, named.shape[0]):
        chosen = chosen | (named[choice : choice + 1] == expert)
    earlier = (
        lax.broadcasted_iota(jnp.int32, (rows, rows), 0)
        < lax.broadcasted_iota(jnp.int32, (rows, rows), 1)
    ).astype(jnp.float32)
    before = jnp.dot(
        chosen.astype(jnp.float32).astype(jnp.bfloat16),
        earlier.astype(jnp.bfloat16),
        preferred_element_type=jnp.float32,
    )
    place = jnp.where(chosen, before, -1.0).astype(jnp.int32)
    slot = lax.broadcasted_iota(jnp.int32, (CAPACITY, rows), 0)
    copies = []
    for j in range(EXPERTS):
        select = (place[j : j + 1] == slot).astype(jnp.float32).astype(jnp.bfloat16)
        start = 0
        for value_ref in values:
            width = value_ref.shape[2]
            buffer[j, :, start : start + width] = jnp.dot(
                select, value_ref[0], preferred_element_type=jnp.float32
            ).astype(jnp.bfloat16)
            start += width
        for i in range(out.shape[0]):
            for k in range(out.shape[2]):
                copy = pltpu.make_async_copy(
                    buffer.at[j], out.at[i, j, k], semaphores.at[len(copies)]
                )
                copy.start()
                copies.append(copy)
    for copy in copies:
        copy.wait()


def pick(step, plan, routes, values, n_xhi, per_expert):
    width = sum(value.shape[2] for value, _ in values)
    specs = [pl.BlockSpec((1,) + routes.shape[1:], lambda i, p: (p[step], 0, 0))]
    for value, planned in values:
        if planned:
            specs.append(pl.BlockSpec((1,) + value.shape[1:], lambda i, p: (p[step], 0, 0)))
        else:
            specs.append(pl.BlockSpec((1,) + value.shape[1:], lambda i, p: (0, 0, 0)))
    out = pl.pallas_call(
        pick_kernel,
        out_shape=jax.ShapeDtypeStruct(
            (n_xhi, EXPERTS, per_expert, CAPACITY, width), jnp.bfloat16
        ),
        grid_spec=pltpu.PrefetchScalarGridSpec(
            num_scalar_prefetch=1,
            grid=(1,),
            in_specs=specs,
            out_specs=pl.BlockSpec(memory_space=pltpu.HBM),
            scratch_shapes=[
                pltpu.VMEM((EXPERTS, CAPACITY, width), jnp.bfloat16),
                pltpu.SemaphoreType.DMA((n_xhi * EXPERTS * per_expert,)),
            ],
        ),
        compiler_params=pltpu.CompilerParams(dimension_semantics=("arbitrary",)),
        name="pick",
    )(plan, routes, *[value for value, _ in values])
    return out.reshape(n_xhi * EXPERTS * per_expert, CAPACITY, width)


def landed(value):
    anywhere = pl.BlockSpec(memory_space=pltpu.HBM)
    return pl.pallas_call(
        lambda value_ref, same_ref: None,
        out_shape=jax.ShapeDtypeStruct(value.shape, value.dtype),
        in_specs=[anywhere],
        out_specs=anywhere,
        input_output_aliases={0: 0},
        cost_estimate=pl.CostEstimate(
            flops=10**11, transcendentals=0, bytes_accessed=10**8
        ),
        name="landed",
    )(value)


def slots(route_now, share_now):
    rows = route_now.shape[0]
    named = route_now.T[None] == jnp.arange(EXPERTS, dtype=jnp.int32)[:, None, None]
    chosen = jnp.any(named, axis=1)
    mix = jnp.sum(jnp.where(named, share_now.T[None], 0.0), axis=1)
    token = jnp.arange(rows, dtype=jnp.int32)
    earlier = (token[:, None] < token[None, :]).astype(jnp.bfloat16)
    before = jnp.dot(
        chosen.astype(jnp.bfloat16), earlier, preferred_element_type=jnp.float32
    ).astype(jnp.int32)
    place = jnp.where(chosen, before, -1)
    hit = place[:, None, :] == jnp.arange(CAPACITY, dtype=jnp.int32)[None, :, None]
    mixing = jnp.where(hit, mix[:, None, :], 0.0).reshape(EXPERTS * CAPACITY, rows)
    return mixing


def per_device(grad_in, saved_input, routes, route_weights, plan, up_weight, down_weight):
    n_expert = lax.axis_size("expert")
    n_xhi = lax.axis_size("xhi")
    n_section = lax.axis_size("section")
    per_expert = n_expert // EXPERTS
    peers = n_xhi * n_expert
    rows, quarter = grad_in.shape[1:]
    up_local = pltpu.with_memory_space_constraint(up_weight[0], pltpu.HBM)
    down_local = pltpu.with_memory_space_constraint(down_weight[0], pltpu.HBM)
    core = lax.axis_index("core").astype(jnp.int32).reshape(1)

    def swap_cores(value):
        return lax.ppermute(value, "core", [(0, 1), (1, 0)])

    def exchange(value):
        return lax.all_to_all(value, ("xhi", "expert"), split_axis=0, concat_axis=0, tiled=True)

    def deliver(sent):
        return exchange(sent).reshape(n_xhi, n_expert * CAPACITY, sent.shape[2])

    def combine(current, mixing, arrived):
        summed = jnp.sum(
            arrived.reshape(n_xhi, EXPERTS, per_expert, CAPACITY, quarter).astype(jnp.float32),
            axis=(0, 2),
        )
        moe_term = lax.dot_general(
            mixing,
            summed.reshape(EXPERTS * CAPACITY, quarter),
            (((0,), (0,)), ((), ())),
            precision=lax.Precision.HIGHEST,
            preferred_element_type=jnp.float32,
        )
        result = (current.astype(jnp.float32) + moe_term).astype(jnp.bfloat16)
        return lax.ppermute(
            result, "section", [(i, (i - 1) % n_section) for i in range(n_section)]
        )

    def outgoing(send, keep):
        return (
            keep.astype(jnp.float32) + swap_cores(send).astype(jnp.float32)
        ).astype(jnp.bfloat16).reshape(peers, CAPACITY, quarter)

    micros = plan[0]
    routes_by_choice = routes[0].transpose(0, 2, 1)
    saved_all = saved_input[0]
    current = grad_in[0]
    ticks = micros.shape[0]

    def mixing_of(tick):
        route_now = lax.dynamic_index_in_dim(routes[0], micros[tick], 0, keepdims=False)
        share_now = lax.dynamic_index_in_dim(route_weights[0], micros[tick], 0, keepdims=False)
        return slots(route_now, share_now)

    def pick_rows(tick, *values):
        return pick(tick, micros, routes_by_choice, values, n_xhi, per_expert)

    rows_in = deliver(pick_rows(0, (saved_all, True), (current[None], False)))
    later = None
    for tick in range(ticks):
        if tick == 0:
            both, swapped = rows_in, None
            if ticks > 1:
                saved_sent, both = together(pick_rows(1, (saved_all, True)), both)
                later = deliver(saved_sent)
            swapped = swap_cores(both)
            saved, grads = (both, swapped, 0), (both, swapped, 1)
            factors = factor(core, saved, up_local)
        else:
            grad_sent, later = together(pick_rows(tick, (current[None], False)), later)
            grad_rows = deliver(grad_sent)
            factors = factor(core, (later, swap_cores(later), 0), up_local)
            grad_rows, factors = together(grad_rows, factors)
            grads = (grad_rows, swap_cores(grad_rows), 0)
        complete = tick + 1 < ticks
        made = sent_part(core, grads, down_local, factors, up_local, complete)
        if complete:
            send, keep = made
        else:
            grad_pre, send = made
            keep = kept_part(core, grad_pre, up_local)
        got = swap_cores(send)
        if tick + 1 < ticks:
            keep, later = together(keep, landed(later))
        partial_rows = (keep.astype(jnp.float32) + got.astype(jnp.float32)).astype(jnp.bfloat16)
        arrived = exchange(partial_rows.reshape(peers, CAPACITY, quarter))
        current = combine(current, mixing_of(tick), arrived)
    return current[None]


def solution(mesh):
    sections, experts, parts = (mesh.shape[name] for name in ("section", "expert", "mp"))
    refined = Mesh(
        mesh.devices.reshape(sections, experts, parts // 2, 2),
        ("section", "expert", "xhi", "core"),
    )
    mp = ("xhi", "core")
    placed = (
        P("section", "expert", mp),
        P("section", None, "expert", mp),
        P("section", None, "expert", None),
        P("section", None, "expert", None),
        P("section", None),
        P("section", None, ("expert", "xhi", "core")),
        P("section", ("expert", "xhi", "core"), None),
    )
    return jax.shard_map(
        per_device,
        mesh=refined,
        in_specs=placed,
        out_specs=P("section", "expert", mp),
        check_vma=False,
    )
```

```python
import jax
import jax.numpy as jnp
from jax import lax
from jax.experimental import pallas as pl
from jax.experimental.pallas import tpu as pltpu
from jax.sharding import Mesh, PartitionSpec as P

EXPERTS = 4
CAPACITY = 72
HIDDEN_BLOCK = 256
VMEM_LIMIT = 18 * 1024 * 1024


def together(*values):
    return lax.optimization_barrier(values)


def contract_last(left, right):
    return lax.dot_general(
        left, right, (((1,), (1,)), ((), ())), preferred_element_type=jnp.float32
    )


HBM_SPEC = pl.BlockSpec(memory_space=pltpu.HBM)
VMEM_SPEC = pl.BlockSpec(memory_space=pltpu.VMEM)


def local_kernel(kernel, name, core, far, near, outs, scratch, flops=1000):
    return pl.pallas_call(
        kernel,
        out_shape=tuple(shape for shape, _ in outs),
        in_specs=[pl.BlockSpec(memory_space=pltpu.SMEM)]
        + [HBM_SPEC] * len(far)
        + [VMEM_SPEC] * len(near),
        out_specs=tuple(place for _, place in outs),
        scratch_shapes=scratch,
        compiler_params=pltpu.CompilerParams(vmem_limit_bytes=VMEM_LIMIT),
        cost_estimate=pl.CostEstimate(flops=flops, transcendentals=0, bytes_accessed=1000),
        name=name,
    )(core, *far, *near)


def stage_kernel(up, down, up_out, down_out, semaphores):
    pieces = semaphores.shape[0] // 2
    copies = []
    for source, target in ((up, up_out), (down, down_out)):
        step = source.shape[0] // pieces
        for piece in range(pieces):
            part = pl.ds(piece * step, step)
            copies.append(
                pltpu.make_async_copy(
                    source.at[part], target.at[part], semaphores.at[len(copies)]
                )
            )
            copies[-1].start()
    for copy in copies:
        copy.wait()


def stage(up, down, name):
    return pl.pallas_call(
        stage_kernel,
        out_shape=(pltpu.VMEM(up.shape, up.dtype), pltpu.VMEM(down.shape, down.dtype)),
        in_specs=[HBM_SPEC, HBM_SPEC],
        out_specs=(VMEM_SPEC, VMEM_SPEC),
        scratch_shapes=[pltpu.SemaphoreType.DMA((8,))],
        compiler_params=pltpu.CompilerParams(vmem_limit_bytes=1024 * 1024),
        cost_estimate=pl.CostEstimate(flops=1000, transcendentals=0, bytes_accessed=1000),
        name=name,
    )(up, down)


def row_copies(sources, column, rows_buf, semaphores):
    quarter = rows_buf.shape[2]
    halves = sources[0].shape[0]
    copies = [
        pltpu.make_async_copy(
            source.at[xhi, :, pl.ds(column * quarter, quarter)],
            rows_buf.at[n * halves + xhi],
            semaphores.at[n * halves + xhi],
        )
        for n, source in enumerate(sources)
        for xhi in range(halves)
    ]
    for copy in copies:
        copy.start()
    return copies


def first_feature(number, halves, core, quarter):
    side = core if number < halves else 1 - core
    return pl.multiple_of((2 * (number % halves) + side) * quarter, quarter)


def hidden_blocks(hidden):
    return [slice(start, start + HIDDEN_BLOCK) for start in range(0, hidden, HIDDEN_BLOCK)]


def factor_kernel(column, core_ref, mine, other, up, out, rows_buf, semaphores):
    copies = row_copies((mine, other), column, rows_buf, semaphores)
    pieces, _, quarter = rows_buf.shape
    for copy in copies:
        copy.wait()
    for block in hidden_blocks(up.shape[1]):
        pre = None
        for number in range(pieces):
            first = first_feature(number, pieces // 2, core_ref[0], quarter)
            part = jnp.dot(
                rows_buf[number],
                up[pl.ds(first, quarter), block],
                preferred_element_type=jnp.float32,
            )
            pre = part if pre is None else pre + part
        sigma = jax.nn.sigmoid(pre)
        out[:, block] = sigma * (1.0 + pre * (1.0 - sigma))


def factor(core, saved, up):
    mine, other, column = saved
    halves, rows = mine.shape[:2]
    width, hidden = up.shape
    pieces = 2 * halves
    return local_kernel(
        lambda *refs: factor_kernel(column, *refs),
        "factor",
        core,
        [mine, other],
        [up],
        [(pltpu.VMEM((rows, hidden), jnp.float32), VMEM_SPEC)],
        [
            pltpu.VMEM((pieces, rows, width // pieces), jnp.bfloat16),
            pltpu.SemaphoreType.DMA((pieces,)),
        ],
    )[0]


def add_act(rows_buf, numbers, core, down, block):
    act = None
    halves = down.shape[1] // rows_buf.shape[2] // 2
    for slot, number in enumerate(numbers):
        first = first_feature(number, halves, core, rows_buf.shape[2])
        part = contract_last(rows_buf[slot], down[block, pl.ds(first, rows_buf.shape[2])])
        act = part if act is None else act + part
    return act


def branch_parts(numbers, core, grad_pre, up, results, targets, semaphores):
    quarter = results.shape[2]
    halves = up.shape[0] // quarter // 2
    sent = []
    for slot, number in enumerate(numbers):
        first = first_feature(number, halves, core, quarter)
        results[slot] = contract_last(
            grad_pre[...], up[pl.ds(first, quarter), :]
        ).astype(jnp.bfloat16)
        copy = pltpu.make_async_copy(results.at[slot], targets[slot], semaphores.at[slot])
        copy.start()
        sent.append(copy)
    for copy in sent:
        copy.wait()


def branch_kernel(
    column, core_ref, mine, other, up, down, factors, send, keep, rows_buf, grad_pre, results,
    semaphores, out_semaphores,
):
    copies = row_copies((mine, other), column, rows_buf, semaphores)
    pieces = rows_buf.shape[0]
    halves = pieces // 2
    for copy in copies:
        copy.wait()
    for block in hidden_blocks(down.shape[0]):
        act = add_act(rows_buf, range(pieces), core_ref[0], down, block)
        grad_pre[:, block] = (act * factors[:, block]).astype(jnp.bfloat16)
    numbers = [halves + n for n in range(halves)] + list(range(halves))
    targets = [send.at[n] for n in range(halves)] + [keep.at[n] for n in range(halves)]
    branch_parts(numbers, core_ref[0], grad_pre, up, results, targets, out_semaphores)


def branch(core, grads, up, down, factors):
    mine, other, column = grads
    halves, rows = mine.shape[:2]
    hidden, width = down.shape
    pieces = 2 * halves
    quarter = width // pieces
    part = (halves, rows, quarter)
    return local_kernel(
        lambda *refs: branch_kernel(column, *refs),
        "branch",
        core,
        [mine, other],
        [up, down, factors],
        [
            (jax.ShapeDtypeStruct(part, jnp.bfloat16), HBM_SPEC),
            (pltpu.HBM(part, jnp.bfloat16), HBM_SPEC),
        ],
        [
            pltpu.VMEM((pieces, rows, quarter), jnp.bfloat16),
            pltpu.VMEM((rows, hidden), jnp.bfloat16),
            pltpu.VMEM((pieces, rows, quarter), jnp.bfloat16),
            pltpu.SemaphoreType.DMA((pieces,)),
            pltpu.SemaphoreType.DMA((pieces,)),
        ],
    )


def own_act_kernel(core_ref, mine, down, out, rows_buf, semaphores):
    for copy in row_copies((mine,), 0, rows_buf, semaphores):
        copy.wait()
    for block in hidden_blocks(down.shape[0]):
        out[:, block] = add_act(rows_buf, range(rows_buf.shape[0]), core_ref[0], down, block)


def own_act(core, mine, down):
    halves, rows, quarter = mine.shape
    return local_kernel(
        own_act_kernel,
        "own_act",
        core,
        [mine],
        [down],
        [(pltpu.VMEM((rows, down.shape[0]), jnp.float32), VMEM_SPEC)],
        [
            pltpu.VMEM((halves, rows, quarter), jnp.bfloat16),
            pltpu.SemaphoreType.DMA((halves,)),
        ],
    )[0]


def sent_kernel(
    core_ref, other, up, down, own, factors, grad_pre, send, rows_buf, results, semaphores,
    out_semaphores,
):
    halves = rows_buf.shape[0]
    late = [halves + n for n in range(halves)]
    for copy in row_copies((other,), 0, rows_buf, semaphores):
        copy.wait()
    for block in hidden_blocks(down.shape[0]):
        act = own[:, block] + add_act(rows_buf, late, core_ref[0], down, block)
        grad_pre[:, block] = (act * factors[:, block]).astype(jnp.bfloat16)
    targets = [send.at[n] for n in range(halves)]
    branch_parts(late, core_ref[0], grad_pre, up, results, targets, out_semaphores)


def sent_part(core, other, up, down, own, factors):
    halves, rows, quarter = other.shape
    return local_kernel(
        sent_kernel,
        "sent_part",
        core,
        [other],
        [up, down, own, factors],
        [
            (pltpu.VMEM((rows, down.shape[0]), jnp.bfloat16), VMEM_SPEC),
            (jax.ShapeDtypeStruct(other.shape, jnp.bfloat16), HBM_SPEC),
        ],
        [
            pltpu.VMEM((halves, rows, quarter), jnp.bfloat16),
            pltpu.VMEM((halves, rows, quarter), jnp.bfloat16),
            pltpu.SemaphoreType.DMA((halves,)),
            pltpu.SemaphoreType.DMA((halves,)),
        ],
    )


def kept_kernel(core_ref, up, grad_pre, keep, results, semaphores):
    halves = keep.shape[0]
    targets = [keep.at[n] for n in range(halves)]
    branch_parts(range(halves), core_ref[0], grad_pre, up, results, targets, semaphores)


def kept_part(core, up, grad_pre, part):
    return local_kernel(
        kept_kernel,
        "kept_part",
        core,
        [],
        [up, grad_pre],
        [(jax.ShapeDtypeStruct(part, jnp.bfloat16), HBM_SPEC)],
        [pltpu.VMEM(part, jnp.bfloat16), pltpu.SemaphoreType.DMA((part[0],))],
        flops=10**10,
    )[0]


def pick_kernel(plan_ref, routes_ref, *refs):
    del plan_ref
    values, (out, buffer, semaphores) = refs[:-3], refs[-3:]
    rows = routes_ref.shape[2]
    expert = lax.broadcasted_iota(jnp.int32, (16, rows), 0)
    named = routes_ref[0]
    chosen = named[0:1] == expert
    for choice in range(1, named.shape[0]):
        chosen = chosen | (named[choice : choice + 1] == expert)
    earlier = (
        lax.broadcasted_iota(jnp.int32, (rows, rows), 0)
        < lax.broadcasted_iota(jnp.int32, (rows, rows), 1)
    ).astype(jnp.float32)
    before = jnp.dot(
        chosen.astype(jnp.float32).astype(jnp.bfloat16),
        earlier.astype(jnp.bfloat16),
        preferred_element_type=jnp.float32,
    )
    place = jnp.where(chosen, before, -1.0).astype(jnp.int32)
    slot = lax.broadcasted_iota(jnp.int32, (CAPACITY, rows), 0)
    copies = []
    for j in range(EXPERTS):
        select = (place[j : j + 1] == slot).astype(jnp.float32).astype(jnp.bfloat16)
        start = 0
        for value_ref in values:
            width = value_ref.shape[2]
            buffer[j, :, start : start + width] = jnp.dot(
                select, value_ref[0], preferred_element_type=jnp.float32
            ).astype(jnp.bfloat16)
            start += width
        for i in range(out.shape[0]):
            for k in range(out.shape[2]):
                copy = pltpu.make_async_copy(
                    buffer.at[j], out.at[i, j, k], semaphores.at[len(copies)]
                )
                copy.start()
                copies.append(copy)
    for copy in copies:
        copy.wait()


def pick(step, plan, routes, values, n_xhi, per_expert):
    width = sum(value.shape[2] for value, _ in values)
    specs = [pl.BlockSpec((1,) + routes.shape[1:], lambda i, p: (p[step], 0, 0))]
    for value, planned in values:
        if planned:
            specs.append(pl.BlockSpec((1,) + value.shape[1:], lambda i, p: (p[step], 0, 0)))
        else:
            specs.append(pl.BlockSpec((1,) + value.shape[1:], lambda i, p: (0, 0, 0)))
    out = pl.pallas_call(
        pick_kernel,
        out_shape=jax.ShapeDtypeStruct(
            (n_xhi, EXPERTS, per_expert, CAPACITY, width), jnp.bfloat16
        ),
        grid_spec=pltpu.PrefetchScalarGridSpec(
            num_scalar_prefetch=1,
            grid=(1,),
            in_specs=specs,
            out_specs=pl.BlockSpec(memory_space=pltpu.HBM),
            scratch_shapes=[
                pltpu.VMEM((EXPERTS, CAPACITY, width), jnp.bfloat16),
                pltpu.SemaphoreType.DMA((n_xhi * EXPERTS * per_expert,)),
            ],
        ),
        compiler_params=pltpu.CompilerParams(dimension_semantics=("arbitrary",)),
        name="pick",
    )(plan, routes, *[value for value, _ in values])
    return out.reshape(n_xhi * EXPERTS * per_expert, CAPACITY, width)


def landed(value):
    anywhere = pl.BlockSpec(memory_space=pltpu.HBM)
    return pl.pallas_call(
        lambda value_ref, same_ref: None,
        out_shape=jax.ShapeDtypeStruct(value.shape, value.dtype),
        in_specs=[anywhere],
        out_specs=anywhere,
        input_output_aliases={0: 0},
        cost_estimate=pl.CostEstimate(
            flops=10**11, transcendentals=0, bytes_accessed=10**8
        ),
        name="landed",
    )(value)


def slots(route_now, share_now):
    rows = route_now.shape[0]
    named = route_now.T[None] == jnp.arange(EXPERTS, dtype=jnp.int32)[:, None, None]
    chosen = jnp.any(named, axis=1)
    mix = jnp.sum(jnp.where(named, share_now.T[None], 0.0), axis=1)
    token = jnp.arange(rows, dtype=jnp.int32)
    earlier = (token[:, None] < token[None, :]).astype(jnp.bfloat16)
    before = jnp.dot(
        chosen.astype(jnp.bfloat16), earlier, preferred_element_type=jnp.float32
    ).astype(jnp.int32)
    place = jnp.where(chosen, before, -1)
    hit = place[:, None, :] == jnp.arange(CAPACITY, dtype=jnp.int32)[None, :, None]
    mixing = jnp.where(hit, mix[:, None, :], 0.0).reshape(EXPERTS * CAPACITY, rows)
    return hit, mixing


def per_device(grad_in, saved_input, routes, route_weights, plan, up_weight, down_weight):
    n_expert = lax.axis_size("expert")
    n_xhi = lax.axis_size("xhi")
    n_section = lax.axis_size("section")
    per_expert = n_expert // EXPERTS
    peers = n_xhi * n_expert
    rows, quarter = grad_in.shape[1:]
    up_local = pltpu.with_memory_space_constraint(up_weight[0], pltpu.HBM)
    down_local = pltpu.with_memory_space_constraint(down_weight[0], pltpu.HBM)
    core = lax.axis_index("core").astype(jnp.int32).reshape(1)

    def swap_cores(value):
        return lax.ppermute(value, "core", [(0, 1), (1, 0)])

    def exchange(value):
        return lax.all_to_all(value, ("xhi", "expert"), split_axis=0, concat_axis=0, tiled=True)

    def deliver(sent):
        return exchange(sent).reshape(n_xhi, n_expert * CAPACITY, sent.shape[2])

    def combine(current, mixing, arrived):
        summed = jnp.sum(
            arrived.reshape(n_xhi, EXPERTS, per_expert, CAPACITY, quarter).astype(jnp.float32),
            axis=(0, 2),
        )
        moe_term = lax.dot_general(
            mixing,
            summed.reshape(EXPERTS * CAPACITY, quarter),
            (((0,), (0,)), ((), ())),
            precision=lax.Precision.HIGHEST,
            preferred_element_type=jnp.float32,
        )
        result = (current.astype(jnp.float32) + moe_term).astype(jnp.bfloat16)
        return lax.ppermute(
            result, "section", [(i, (i - 1) % n_section) for i in range(n_section)]
        )

    def outgoing(send, keep):
        return (
            keep.astype(jnp.float32) + swap_cores(send).astype(jnp.float32)
        ).astype(jnp.bfloat16).reshape(peers, CAPACITY, quarter)

    micros = plan[0]
    routes_by_choice = routes[0].transpose(0, 2, 1)
    saved_all = saved_input[0]
    current = grad_in[0]
    ticks = micros.shape[0]

    def slots_of(tick):
        route_now = lax.dynamic_index_in_dim(routes[0], micros[tick], 0, keepdims=False)
        share_now = lax.dynamic_index_in_dim(route_weights[0], micros[tick], 0, keepdims=False)
        return slots(route_now, share_now)

    def pick_rows(tick, *values):
        return pick(tick, micros, routes_by_choice, values, n_xhi, per_expert)

    both = deliver(pick_rows(0, (saved_all, True), (current[None], False)))
    up_near, down_near = stage(up_local, down_local, "stage_first")
    both, up_near, down_near = together(both, up_near, down_near)
    later = None
    if ticks > 1:
        saved_sent, both = together(pick_rows(1, (saved_all, True)), both)
        later = deliver(saved_sent)
    swapped = swap_cores(both)
    factors = factor(core, (both, swapped, 0), up_near)
    send, keep = branch(core, (both, swapped, 1), up_near, down_near, factors)
    for tick in range(ticks):
        got = swap_cores(send)
        if tick + 1 < ticks:
            keep, later = together(keep, landed(later))
        partial_rows = (keep.astype(jnp.float32) + got.astype(jnp.float32)).astype(jnp.bfloat16)
        arrived = exchange(partial_rows.reshape(peers, CAPACITY, quarter))
        _, mixing = slots_of(tick)
        if tick + 1 == ticks:
            return combine(current, mixing, arrived)[None]
        later_swapped = swap_cores(later)
        hit, _ = slots_of(tick + 1)
        picks = jnp.broadcast_to(
            hit[None, :, None], (n_xhi, EXPERTS, per_expert, CAPACITY, rows)
        ).reshape(peers * CAPACITY, rows)
        arrived, later_swapped, picks = together(arrived, later_swapped, picks)
        current = combine(current, mixing, arrived)
        grad_sent = jnp.dot(
            picks.astype(jnp.bfloat16), current, preferred_element_type=jnp.float32
        ).astype(jnp.bfloat16)
        grad_sent, later, later_swapped = together(
            grad_sent.reshape(peers, CAPACITY, quarter), later, later_swapped
        )
        grad_rows = deliver(grad_sent)
        up_near, down_near = stage(up_local, down_local, "stage_next")
        factors = factor(core, (later, later_swapped, 0), up_near)
        grad_rows, factors, down_near = together(grad_rows, factors, down_near)
        swapped = swap_cores(grad_rows)
        own = own_act(core, grad_rows, down_near)
        grad_pre, send = sent_part(core, swapped, up_near, down_near, own, factors)
        keep = kept_part(core, up_near, grad_pre, send.shape)


def solution(mesh):
    sections, experts, parts = (mesh.shape[name] for name in ("section", "expert", "mp"))
    refined = Mesh(
        mesh.devices.reshape(sections, experts, parts // 2, 2),
        ("section", "expert", "xhi", "core"),
    )
    mp = ("xhi", "core")
    placed = (
        P("section", "expert", mp),
        P("section", None, "expert", mp),
        P("section", None, "expert", None),
        P("section", None, "expert", None),
        P("section", None),
        P("section", None, ("expert", "xhi", "core")),
        P("section", ("expert", "xhi", "core"), None),
    )
    return jax.shard_map(
        per_device,
        mesh=refined,
        in_specs=placed,
        out_specs=P("section", "expert", mp),
        check_vma=False,
    )
```

```python
import jax
import jax.numpy as jnp
from jax import lax
from jax.experimental import pallas as pl
from jax.experimental.pallas import tpu as pltpu
from jax.sharding import Mesh, PartitionSpec as P

EXPERTS = 4
CAPACITY = 72
HIDDEN_BLOCK = 256
VMEM_LIMIT = 22 * 1024 * 1024


def together(*values):
    return lax.optimization_barrier(values)


def contract_last(left, right):
    return lax.dot_general(
        left, right, (((1,), (1,)), ((), ())), preferred_element_type=jnp.float32
    )


HBM_SPEC = pl.BlockSpec(memory_space=pltpu.HBM)
VMEM_SPEC = pl.BlockSpec(memory_space=pltpu.VMEM)


def local_kernel(kernel, name, core, far, near, outs, scratch, flops=1000):
    return pl.pallas_call(
        kernel,
        out_shape=tuple(shape for shape, _ in outs),
        in_specs=[pl.BlockSpec(memory_space=pltpu.SMEM)]
        + [HBM_SPEC] * len(far)
        + [VMEM_SPEC] * len(near),
        out_specs=tuple(place for _, place in outs),
        scratch_shapes=scratch,
        compiler_params=pltpu.CompilerParams(vmem_limit_bytes=VMEM_LIMIT),
        cost_estimate=pl.CostEstimate(flops=flops, transcendentals=0, bytes_accessed=1000),
        name=name,
    )(core, *far, *near)


def row_copies(sources, column, rows_buf, semaphores):
    quarter = rows_buf.shape[2]
    halves = sources[0].shape[0]
    copies = [
        pltpu.make_async_copy(
            source.at[xhi, :, pl.ds(column * quarter, quarter)],
            rows_buf.at[n * halves + xhi],
            semaphores.at[n * halves + xhi],
        )
        for n, source in enumerate(sources)
        for xhi in range(halves)
    ]
    for copy in copies:
        copy.start()
    return copies


def first_feature(number, halves, core, quarter):
    side = core if number < halves else 1 - core
    return pl.multiple_of((2 * (number % halves) + side) * quarter, quarter)


def hidden_blocks(hidden):
    return [slice(start, start + HIDDEN_BLOCK) for start in range(0, hidden, HIDDEN_BLOCK)]


def factor_kernel(column, core_ref, mine, other, up, out, rows_buf, up_buf, semaphores):
    pieces, _, quarter = rows_buf.shape
    copies = row_copies((mine, other), column, rows_buf, semaphores)
    for number in range(pieces):
        first = first_feature(number, pieces // 2, core_ref[0], quarter)
        copies.append(
            pltpu.make_async_copy(
                up.at[pl.ds(first, quarter), :], up_buf.at[number], semaphores.at[pieces + number]
            )
        )
        copies[-1].start()
    for number in range(pieces):
        copies[number].wait()
        copies[pieces + number].wait()
        for block in hidden_blocks(up.shape[1]):
            part = jnp.dot(
                rows_buf[number], up_buf[number, :, block], preferred_element_type=jnp.float32
            )
            if number:
                part = out[:, block] + part
            if number + 1 == pieces:
                sigma = jax.nn.sigmoid(part)
                part = sigma * (1.0 + part * (1.0 - sigma))
            out[:, block] = part


def factor(core, saved, up):
    mine, other, column = saved
    halves, rows = mine.shape[:2]
    width, hidden = up.shape
    pieces = 2 * halves
    return local_kernel(
        lambda *refs: factor_kernel(column, *refs),
        "factor",
        core,
        [mine, other, up],
        [],
        [(pltpu.VMEM((rows, hidden), jnp.float32), VMEM_SPEC)],
        [
            pltpu.VMEM((pieces, rows, width // pieces), jnp.bfloat16),
            pltpu.VMEM((pieces, width // pieces, hidden), jnp.bfloat16),
            pltpu.SemaphoreType.DMA((2 * pieces,)),
        ],
    )[0]


def act_sums(sources, column, numbers, core, down, rows_buf, down_buf, semaphores):
    quarter = rows_buf.shape[2]
    copies = row_copies(sources, column, rows_buf, semaphores)
    count = len(numbers)
    for slot, number in enumerate(numbers):
        first = first_feature(number, sources[0].shape[0], core, quarter)
        copies.append(
            pltpu.make_async_copy(
                down.at[:, pl.ds(first, quarter)],
                down_buf.at[slot],
                semaphores.at[count + slot],
            )
        )
        copies[-1].start()
    for slot in range(count):
        copies[slot].wait()
        copies[count + slot].wait()
        for block in hidden_blocks(down.shape[0]):
            yield slot, block, contract_last(rows_buf[slot], down_buf[slot, block, :])


def branch_parts(numbers, core, grad_pre, up, results, targets, semaphores):
    quarter = results.shape[2]
    halves = up.shape[0] // quarter // 2
    sent = []
    for slot, number in enumerate(numbers):
        first = first_feature(number, halves, core, quarter)
        results[slot] = contract_last(
            grad_pre[...], up[pl.ds(first, quarter), :]
        ).astype(jnp.bfloat16)
        copy = pltpu.make_async_copy(results.at[slot], targets[slot], semaphores.at[slot])
        copy.start()
        sent.append(copy)
    for copy in sent:
        copy.wait()


def branch_kernel(
    column, core_ref, mine, other, down, up, factors, send, keep, rows_buf, down_buf, acc,
    grad_pre, results, semaphores, out_semaphores,
):
    pieces = rows_buf.shape[0]
    halves = pieces // 2
    for slot, block, part in act_sums(
        (mine, other), column, range(pieces), core_ref[0], down, rows_buf, down_buf, semaphores
    ):
        total = acc[:, block] + part if slot else part
        if slot + 1 < pieces:
            acc[:, block] = total
        else:
            grad_pre[:, block] = (total * factors[:, block]).astype(jnp.bfloat16)
    numbers = [halves + n for n in range(halves)] + list(range(halves))
    targets = [send.at[n] for n in range(halves)] + [keep.at[n] for n in range(halves)]
    branch_parts(numbers, core_ref[0], grad_pre, up, results, targets, out_semaphores)


def act_buffers(pieces, rows, quarter, hidden):
    return [
        pltpu.VMEM((pieces, rows, quarter), jnp.bfloat16),
        pltpu.VMEM((pieces, hidden, quarter), jnp.bfloat16),
    ]


def branch(core, grads, up, down, factors):
    mine, other, column = grads
    halves, rows = mine.shape[:2]
    hidden, width = down.shape
    pieces = 2 * halves
    quarter = width // pieces
    part = (halves, rows, quarter)
    return local_kernel(
        lambda *refs: branch_kernel(column, *refs),
        "branch",
        core,
        [mine, other, down],
        [up, factors],
        [
            (jax.ShapeDtypeStruct(part, jnp.bfloat16), HBM_SPEC),
            (pltpu.HBM(part, jnp.bfloat16), HBM_SPEC),
        ],
        act_buffers(pieces, rows, quarter, hidden)
        + [
            pltpu.VMEM((rows, hidden), jnp.float32),
            pltpu.VMEM((rows, hidden), jnp.bfloat16),
            pltpu.VMEM((pieces, rows, quarter), jnp.bfloat16),
            pltpu.SemaphoreType.DMA((2 * pieces,)),
            pltpu.SemaphoreType.DMA((pieces,)),
        ],
    )


def own_act_kernel(core_ref, mine, down, out, rows_buf, down_buf, semaphores):
    for slot, block, part in act_sums(
        (mine,), 0, range(mine.shape[0]), core_ref[0], down, rows_buf, down_buf, semaphores
    ):
        out[:, block] = out[:, block] + part if slot else part


def own_act(core, mine, down):
    halves, rows, quarter = mine.shape
    return local_kernel(
        own_act_kernel,
        "own_act",
        core,
        [mine, down],
        [],
        [(pltpu.VMEM((rows, down.shape[0]), jnp.float32), VMEM_SPEC)],
        act_buffers(halves, rows, quarter, down.shape[0])
        + [pltpu.SemaphoreType.DMA((2 * halves,))],
    )[0]


def sent_kernel(
    core_ref, other, down, up, own, factors, grad_pre, send, rows_buf, down_buf, acc, results,
    semaphores, out_semaphores,
):
    halves = rows_buf.shape[0]
    late = [halves + n for n in range(halves)]
    for slot, block, part in act_sums(
        (other,), 0, late, core_ref[0], down, rows_buf, down_buf, semaphores
    ):
        total = (acc if slot else own)[:, block] + part
        if slot + 1 < halves:
            acc[:, block] = total
        else:
            grad_pre[:, block] = (total * factors[:, block]).astype(jnp.bfloat16)
    targets = [send.at[n] for n in range(halves)]
    branch_parts(late, core_ref[0], grad_pre, up, results, targets, out_semaphores)


def sent_part(core, other, up, down, own, factors):
    halves, rows, quarter = other.shape
    hidden = down.shape[0]
    return local_kernel(
        sent_kernel,
        "sent_part",
        core,
        [other, down],
        [up, own, factors],
        [
            (pltpu.VMEM((rows, hidden), jnp.bfloat16), VMEM_SPEC),
            (jax.ShapeDtypeStruct(other.shape, jnp.bfloat16), HBM_SPEC),
        ],
        act_buffers(halves, rows, quarter, hidden)
        + [
            pltpu.VMEM((rows, hidden), jnp.float32),
            pltpu.VMEM((halves, rows, quarter), jnp.bfloat16),
            pltpu.SemaphoreType.DMA((2 * halves,)),
            pltpu.SemaphoreType.DMA((halves,)),
        ],
    )


def kept_kernel(core_ref, up, grad_pre, keep, results, semaphores):
    halves = keep.shape[0]
    targets = [keep.at[n] for n in range(halves)]
    branch_parts(range(halves), core_ref[0], grad_pre, up, results, targets, semaphores)


def kept_part(core, up, grad_pre, part):
    return local_kernel(
        kept_kernel,
        "kept_part",
        core,
        [],
        [up, grad_pre],
        [(jax.ShapeDtypeStruct(part, jnp.bfloat16), HBM_SPEC)],
        [pltpu.VMEM(part, jnp.bfloat16), pltpu.SemaphoreType.DMA((part[0],))],
        flops=10**10,
    )[0]


def pick_kernel(plan_ref, routes_ref, *refs):
    del plan_ref
    values, (out, buffer, semaphores) = refs[:-3], refs[-3:]
    rows = routes_ref.shape[2]
    expert = lax.broadcasted_iota(jnp.int32, (16, rows), 0)
    named = routes_ref[0]
    chosen = named[0:1] == expert
    for choice in range(1, named.shape[0]):
        chosen = chosen | (named[choice : choice + 1] == expert)
    earlier = (
        lax.broadcasted_iota(jnp.int32, (rows, rows), 0)
        < lax.broadcasted_iota(jnp.int32, (rows, rows), 1)
    ).astype(jnp.float32)
    before = jnp.dot(
        chosen.astype(jnp.float32).astype(jnp.bfloat16),
        earlier.astype(jnp.bfloat16),
        preferred_element_type=jnp.float32,
    )
    place = jnp.where(chosen, before, -1.0).astype(jnp.int32)
    slot = lax.broadcasted_iota(jnp.int32, (CAPACITY, rows), 0)
    copies = []
    for j in range(EXPERTS):
        select = (place[j : j + 1] == slot).astype(jnp.float32).astype(jnp.bfloat16)
        start = 0
        for value_ref in values:
            width = value_ref.shape[2]
            buffer[j, :, start : start + width] = jnp.dot(
                select, value_ref[0], preferred_element_type=jnp.float32
            ).astype(jnp.bfloat16)
            start += width
        for i in range(out.shape[0]):
            for k in range(out.shape[2]):
                copy = pltpu.make_async_copy(
                    buffer.at[j], out.at[i, j, k], semaphores.at[len(copies)]
                )
                copy.start()
                copies.append(copy)
    for copy in copies:
        copy.wait()


def pick(step, plan, routes, values, n_xhi, per_expert):
    width = sum(value.shape[2] for value, _ in values)
    specs = [pl.BlockSpec((1,) + routes.shape[1:], lambda i, p: (p[step], 0, 0))]
    for value, planned in values:
        if planned:
            specs.append(pl.BlockSpec((1,) + value.shape[1:], lambda i, p: (p[step], 0, 0)))
        else:
            specs.append(pl.BlockSpec((1,) + value.shape[1:], lambda i, p: (0, 0, 0)))
    out = pl.pallas_call(
        pick_kernel,
        out_shape=jax.ShapeDtypeStruct(
            (n_xhi, EXPERTS, per_expert, CAPACITY, width), jnp.bfloat16
        ),
        grid_spec=pltpu.PrefetchScalarGridSpec(
            num_scalar_prefetch=1,
            grid=(1,),
            in_specs=specs,
            out_specs=pl.BlockSpec(memory_space=pltpu.HBM),
            scratch_shapes=[
                pltpu.VMEM((EXPERTS, CAPACITY, width), jnp.bfloat16),
                pltpu.SemaphoreType.DMA((n_xhi * EXPERTS * per_expert,)),
            ],
        ),
        compiler_params=pltpu.CompilerParams(dimension_semantics=("arbitrary",)),
        name="pick",
    )(plan, routes, *[value for value, _ in values])
    return out.reshape(n_xhi * EXPERTS * per_expert, CAPACITY, width)


def landed(value):
    anywhere = pl.BlockSpec(memory_space=pltpu.HBM)
    return pl.pallas_call(
        lambda value_ref, same_ref: None,
        out_shape=jax.ShapeDtypeStruct(value.shape, value.dtype),
        in_specs=[anywhere],
        out_specs=anywhere,
        input_output_aliases={0: 0},
        cost_estimate=pl.CostEstimate(
            flops=10**11, transcendentals=0, bytes_accessed=10**8
        ),
        name="landed",
    )(value)


def slots(route_now, share_now):
    rows = route_now.shape[0]
    named = route_now.T[None] == jnp.arange(EXPERTS, dtype=jnp.int32)[:, None, None]
    chosen = jnp.any(named, axis=1)
    mix = jnp.sum(jnp.where(named, share_now.T[None], 0.0), axis=1)
    token = jnp.arange(rows, dtype=jnp.int32)
    earlier = (token[:, None] < token[None, :]).astype(jnp.bfloat16)
    before = jnp.dot(
        chosen.astype(jnp.bfloat16), earlier, preferred_element_type=jnp.float32
    ).astype(jnp.int32)
    place = jnp.where(chosen, before, -1)
    hit = place[:, None, :] == jnp.arange(CAPACITY, dtype=jnp.int32)[None, :, None]
    mixing = jnp.where(hit, mix[:, None, :], 0.0).reshape(EXPERTS * CAPACITY, rows)
    return hit, mixing


def per_device(grad_in, saved_input, routes, route_weights, plan, up_weight, down_weight):
    n_expert = lax.axis_size("expert")
    n_xhi = lax.axis_size("xhi")
    n_section = lax.axis_size("section")
    per_expert = n_expert // EXPERTS
    peers = n_xhi * n_expert
    rows, quarter = grad_in.shape[1:]
    up_near = up_weight[0]
    up_far = pltpu.with_memory_space_constraint(up_near, pltpu.HBM)
    down_far = pltpu.with_memory_space_constraint(down_weight[0], pltpu.HBM)
    core = lax.axis_index("core").astype(jnp.int32).reshape(1)

    def swap_cores(value):
        return lax.ppermute(value, "core", [(0, 1), (1, 0)])

    def exchange(value):
        return lax.all_to_all(value, ("xhi", "expert"), split_axis=0, concat_axis=0, tiled=True)

    def deliver(sent):
        return exchange(sent).reshape(n_xhi, n_expert * CAPACITY, sent.shape[2])

    def combine(current, mixing, arrived):
        summed = jnp.sum(
            arrived.reshape(n_xhi, EXPERTS, per_expert, CAPACITY, quarter).astype(jnp.float32),
            axis=(0, 2),
        )
        moe_term = lax.dot_general(
            mixing,
            summed.reshape(EXPERTS * CAPACITY, quarter),
            (((0,), (0,)), ((), ())),
            precision=lax.Precision.HIGHEST,
            preferred_element_type=jnp.float32,
        )
        result = (current.astype(jnp.float32) + moe_term).astype(jnp.bfloat16)
        return lax.ppermute(
            result, "section", [(i, (i - 1) % n_section) for i in range(n_section)]
        )

    def outgoing(send, keep):
        return (
            keep.astype(jnp.float32) + swap_cores(send).astype(jnp.float32)
        ).astype(jnp.bfloat16).reshape(peers, CAPACITY, quarter)

    micros = plan[0]
    routes_by_choice = routes[0].transpose(0, 2, 1)
    saved_all = saved_input[0]
    current = grad_in[0]
    ticks = micros.shape[0]

    def slots_of(tick):
        route_now = lax.dynamic_index_in_dim(routes[0], micros[tick], 0, keepdims=False)
        share_now = lax.dynamic_index_in_dim(route_weights[0], micros[tick], 0, keepdims=False)
        return slots(route_now, share_now)

    def pick_rows(tick, *values):
        return pick(tick, micros, routes_by_choice, values, n_xhi, per_expert)

    both = deliver(pick_rows(0, (saved_all, True), (current[None], False)))
    later = None
    if ticks > 1:
        saved_sent, both = together(pick_rows(1, (saved_all, True)), both)
        later = deliver(saved_sent)
    swapped = swap_cores(both)
    factors = factor(core, (both, swapped, 0), up_far)
    send, keep = branch(core, (both, swapped, 1), up_near, down_far, factors)
    for tick in range(ticks):
        got = swap_cores(send)
        if tick + 1 < ticks:
            keep, later = together(keep, landed(later))
        partial_rows = (keep.astype(jnp.float32) + got.astype(jnp.float32)).astype(jnp.bfloat16)
        partial_rows = partial_rows.reshape(peers, CAPACITY, quarter)
        if tick + 1 < ticks:
            partial_rows, later = together(partial_rows, later)
        arrived = exchange(partial_rows)
        _, mixing = slots_of(tick)
        if tick + 1 == ticks:
            return combine(current, mixing, arrived)[None]
        factors = factor(core, (later, swap_cores(later), 0), up_far)
        hit, _ = slots_of(tick + 1)
        picks = jnp.broadcast_to(
            hit[None, :, None], (n_xhi, EXPERTS, per_expert, CAPACITY, rows)
        ).reshape(peers * CAPACITY, rows)
        arrived, factors, picks = together(arrived, factors, picks)
        current = combine(current, mixing, arrived)
        grad_sent = jnp.dot(
            picks.astype(jnp.bfloat16), current, preferred_element_type=jnp.float32
        ).astype(jnp.bfloat16)
        grad_rows = deliver(grad_sent.reshape(peers, CAPACITY, quarter))
        swapped = swap_cores(grad_rows)
        own = own_act(core, grad_rows, down_far)
        grad_pre, send = sent_part(core, swapped, up_near, down_far, own, factors)
        keep = kept_part(core, up_near, grad_pre, send.shape)


def solution(mesh):
    sections, experts, parts = (mesh.shape[name] for name in ("section", "expert", "mp"))
    refined = Mesh(
        mesh.devices.reshape(sections, experts, parts // 2, 2),
        ("section", "expert", "xhi", "core"),
    )
    mp = ("xhi", "core")
    placed = (
        P("section", "expert", mp),
        P("section", None, "expert", mp),
        P("section", None, "expert", None),
        P("section", None, "expert", None),
        P("section", None),
        P("section", None, ("expert", "xhi", "core")),
        P("section", ("expert", "xhi", "core"), None),
    )
    return jax.shard_map(
        per_device,
        mesh=refined,
        in_specs=placed,
        out_specs=P("section", "expert", mp),
        check_vma=False,
    )
```

```python
import jax
import jax.numpy as jnp
from jax import lax
from jax.experimental import pallas as pl
from jax.experimental.pallas import tpu as pltpu
from jax.sharding import Mesh, PartitionSpec as P

EXPERTS = 4
CAPACITY = 72
HIDDEN_BLOCK = 256
VMEM_LIMIT = 22 * 1024 * 1024


def together(*values):
    return lax.optimization_barrier(values)


def contract_last(left, right):
    return lax.dot_general(
        left, right, (((1,), (1,)), ((), ())), preferred_element_type=jnp.float32
    )


HBM_SPEC = pl.BlockSpec(memory_space=pltpu.HBM)
VMEM_SPEC = pl.BlockSpec(memory_space=pltpu.VMEM)


def local_kernel(kernel, name, core, far, near, outs, scratch, flops=1000):
    return pl.pallas_call(
        kernel,
        out_shape=tuple(shape for shape, _ in outs),
        in_specs=[pl.BlockSpec(memory_space=pltpu.SMEM)]
        + [HBM_SPEC] * len(far)
        + [VMEM_SPEC] * len(near),
        out_specs=tuple(place for _, place in outs),
        scratch_shapes=scratch,
        compiler_params=pltpu.CompilerParams(vmem_limit_bytes=VMEM_LIMIT),
        cost_estimate=pl.CostEstimate(flops=flops, transcendentals=0, bytes_accessed=1000),
        name=name,
    )(core, *far, *near)


def row_copies(sources, column, rows_buf, semaphores):
    quarter = rows_buf.shape[2]
    halves = sources[0].shape[0]
    copies = [
        pltpu.make_async_copy(
            source.at[xhi, :, pl.ds(column * quarter, quarter)],
            rows_buf.at[n * halves + xhi],
            semaphores.at[n * halves + xhi],
        )
        for n, source in enumerate(sources)
        for xhi in range(halves)
    ]
    for copy in copies:
        copy.start()
    return copies


def first_feature(number, halves, core, quarter):
    side = core if number < halves else 1 - core
    return pl.multiple_of((2 * (number % halves) + side) * quarter, quarter)


def hidden_blocks(hidden):
    return [slice(start, start + HIDDEN_BLOCK) for start in range(0, hidden, HIDDEN_BLOCK)]


def factor_kernel(column, core_ref, mine, other, up, out, rows_buf, up_buf, semaphores):
    pieces, _, quarter = rows_buf.shape
    copies = row_copies((mine, other), column, rows_buf, semaphores)
    for number in range(pieces):
        first = first_feature(number, pieces // 2, core_ref[0], quarter)
        copies.append(
            pltpu.make_async_copy(
                up.at[pl.ds(first, quarter), :], up_buf.at[number], semaphores.at[pieces + number]
            )
        )
        copies[-1].start()
    for number in range(pieces):
        copies[number].wait()
        copies[pieces + number].wait()
        for block in hidden_blocks(up.shape[1]):
            part = jnp.dot(
                rows_buf[number], up_buf[number, :, block], preferred_element_type=jnp.float32
            )
            if number:
                part = out[:, block] + part
            if number + 1 == pieces:
                sigma = jax.nn.sigmoid(part)
                part = sigma * (1.0 + part * (1.0 - sigma))
            out[:, block] = part


def factor(core, saved, up):
    mine, other, column = saved
    halves, rows = mine.shape[:2]
    width, hidden = up.shape
    pieces = 2 * halves
    return local_kernel(
        lambda *refs: factor_kernel(column, *refs),
        "factor",
        core,
        [mine, other, up],
        [],
        [(pltpu.VMEM((rows, hidden), jnp.float32), VMEM_SPEC)],
        [
            pltpu.VMEM((pieces, rows, width // pieces), jnp.bfloat16),
            pltpu.VMEM((pieces, width // pieces, hidden), jnp.bfloat16),
            pltpu.SemaphoreType.DMA((2 * pieces,)),
        ],
    )[0]


def act_sums(sources, column, numbers, core, down, rows_buf, down_buf, semaphores):
    quarter = rows_buf.shape[2]
    copies = row_copies(sources, column, rows_buf, semaphores)
    count = len(numbers)
    for slot, number in enumerate(numbers):
        first = first_feature(number, sources[0].shape[0], core, quarter)
        copies.append(
            pltpu.make_async_copy(
                down.at[:, pl.ds(first, quarter)],
                down_buf.at[slot],
                semaphores.at[count + slot],
            )
        )
        copies[-1].start()
    for slot in range(count):
        copies[slot].wait()
        copies[count + slot].wait()
        for block in hidden_blocks(down.shape[0]):
            yield slot, block, contract_last(rows_buf[slot], down_buf[slot, block, :])


def up_copies(up, numbers, core, up_buf, semaphores):
    quarter = up_buf.shape[1]
    copies = []
    for slot, number in enumerate(numbers):
        first = first_feature(number, up.shape[0] // quarter // 2, core, quarter)
        copies.append(
            pltpu.make_async_copy(
                up.at[pl.ds(first, quarter), :], up_buf.at[slot], semaphores.at[slot]
            )
        )
        copies[-1].start()
    return copies


def loaded_parts(copies, grad_pre, up_buf, results, targets, semaphores):
    sent = []
    for slot, copy in enumerate(copies):
        copy.wait()
        results[slot] = contract_last(grad_pre[...], up_buf[slot]).astype(jnp.bfloat16)
        sent.append(
            pltpu.make_async_copy(results.at[slot], targets[slot], semaphores.at[slot])
        )
        sent[-1].start()
    for copy in sent:
        copy.wait()


def branch_parts(numbers, core, grad_pre, up, results, targets, semaphores):
    quarter = results.shape[2]
    halves = up.shape[0] // quarter // 2
    sent = []
    for slot, number in enumerate(numbers):
        first = first_feature(number, halves, core, quarter)
        results[slot] = contract_last(
            grad_pre[...], up[pl.ds(first, quarter), :]
        ).astype(jnp.bfloat16)
        copy = pltpu.make_async_copy(results.at[slot], targets[slot], semaphores.at[slot])
        copy.start()
        sent.append(copy)
    for copy in sent:
        copy.wait()


def branch_kernel(
    column, core_ref, mine, other, down, up, factors, send, keep, rows_buf, down_buf, acc,
    grad_pre, results, semaphores, out_semaphores,
):
    pieces = rows_buf.shape[0]
    halves = pieces // 2
    for slot, block, part in act_sums(
        (mine, other), column, range(pieces), core_ref[0], down, rows_buf, down_buf, semaphores
    ):
        total = acc[:, block] + part if slot else part
        if slot + 1 < pieces:
            acc[:, block] = total
        else:
            grad_pre[:, block] = (total * factors[:, block]).astype(jnp.bfloat16)
    numbers = [halves + n for n in range(halves)] + list(range(halves))
    targets = [send.at[n] for n in range(halves)] + [keep.at[n] for n in range(halves)]
    branch_parts(numbers, core_ref[0], grad_pre, up, results, targets, out_semaphores)


def act_buffers(pieces, rows, quarter, hidden):
    return [
        pltpu.VMEM((pieces, rows, quarter), jnp.bfloat16),
        pltpu.VMEM((pieces, hidden, quarter), jnp.bfloat16),
    ]


def branch(core, grads, up, down, factors):
    mine, other, column = grads
    halves, rows = mine.shape[:2]
    hidden, width = down.shape
    pieces = 2 * halves
    quarter = width // pieces
    part = (halves, rows, quarter)
    return local_kernel(
        lambda *refs: branch_kernel(column, *refs),
        "branch",
        core,
        [mine, other, down],
        [up, factors],
        [
            (jax.ShapeDtypeStruct(part, jnp.bfloat16), HBM_SPEC),
            (pltpu.HBM(part, jnp.bfloat16), HBM_SPEC),
        ],
        act_buffers(pieces, rows, quarter, hidden)
        + [
            pltpu.VMEM((rows, hidden), jnp.float32),
            pltpu.VMEM((rows, hidden), jnp.bfloat16),
            pltpu.VMEM((pieces, rows, quarter), jnp.bfloat16),
            pltpu.SemaphoreType.DMA((2 * pieces,)),
            pltpu.SemaphoreType.DMA((pieces,)),
        ],
    )


def own_act_kernel(core_ref, mine, down, out, rows_buf, down_buf, semaphores):
    for slot, block, part in act_sums(
        (mine,), 0, range(mine.shape[0]), core_ref[0], down, rows_buf, down_buf, semaphores
    ):
        out[:, block] = out[:, block] + part if slot else part


def own_act(core, mine, down):
    halves, rows, quarter = mine.shape
    return local_kernel(
        own_act_kernel,
        "own_act",
        core,
        [mine, down],
        [],
        [(pltpu.VMEM((rows, down.shape[0]), jnp.float32), VMEM_SPEC)],
        act_buffers(halves, rows, quarter, down.shape[0])
        + [pltpu.SemaphoreType.DMA((2 * halves,))],
    )[0]


def sent_kernel(
    core_ref, other, down, up, own, factors, grad_pre, send, rows_buf, down_buf, up_buf, acc,
    results, semaphores, up_semaphores, out_semaphores,
):
    halves = rows_buf.shape[0]
    late = [halves + n for n in range(halves)]
    copies = None
    for slot, block, part in act_sums(
        (other,), 0, late, core_ref[0], down, rows_buf, down_buf, semaphores
    ):
        if copies is None:
            copies = up_copies(up, late, core_ref[0], up_buf, up_semaphores)
        total = (acc if slot else own)[:, block] + part
        if slot + 1 < halves:
            acc[:, block] = total
        else:
            grad_pre[:, block] = (total * factors[:, block]).astype(jnp.bfloat16)
    targets = [send.at[n] for n in range(halves)]
    loaded_parts(copies, grad_pre, up_buf, results, targets, out_semaphores)


def sent_part(core, other, up, down, own, factors):
    halves, rows, quarter = other.shape
    hidden = down.shape[0]
    return local_kernel(
        sent_kernel,
        "sent_part",
        core,
        [other, down, up],
        [own, factors],
        [
            (pltpu.VMEM((rows, hidden), jnp.bfloat16), VMEM_SPEC),
            (jax.ShapeDtypeStruct(other.shape, jnp.bfloat16), HBM_SPEC),
        ],
        act_buffers(halves, rows, quarter, hidden)
        + [
            pltpu.VMEM((halves, quarter, hidden), jnp.bfloat16),
            pltpu.VMEM((rows, hidden), jnp.float32),
            pltpu.VMEM((halves, rows, quarter), jnp.bfloat16),
            pltpu.SemaphoreType.DMA((2 * halves,)),
            pltpu.SemaphoreType.DMA((halves,)),
            pltpu.SemaphoreType.DMA((halves,)),
        ],
    )


def kept_kernel(core_ref, up, grad_pre, keep, up_buf, results, up_semaphores, semaphores):
    halves = keep.shape[0]
    copies = up_copies(up, range(halves), core_ref[0], up_buf, up_semaphores)
    targets = [keep.at[n] for n in range(halves)]
    loaded_parts(copies, grad_pre, up_buf, results, targets, semaphores)


def kept_part(core, up, grad_pre, part):
    return local_kernel(
        kept_kernel,
        "kept_part",
        core,
        [up],
        [grad_pre],
        [(jax.ShapeDtypeStruct(part, jnp.bfloat16), HBM_SPEC)],
        [
            pltpu.VMEM((part[0], part[2], up.shape[1]), jnp.bfloat16),
            pltpu.VMEM(part, jnp.bfloat16),
            pltpu.SemaphoreType.DMA((part[0],)),
            pltpu.SemaphoreType.DMA((part[0],)),
        ],
        flops=10**10,
    )[0]


def pick_kernel(plan_ref, routes_ref, *refs):
    del plan_ref
    values, (out, buffer, semaphores) = refs[:-3], refs[-3:]
    rows = routes_ref.shape[2]
    expert = lax.broadcasted_iota(jnp.int32, (16, rows), 0)
    named = routes_ref[0]
    chosen = named[0:1] == expert
    for choice in range(1, named.shape[0]):
        chosen = chosen | (named[choice : choice + 1] == expert)
    earlier = (
        lax.broadcasted_iota(jnp.int32, (rows, rows), 0)
        < lax.broadcasted_iota(jnp.int32, (rows, rows), 1)
    ).astype(jnp.float32)
    before = jnp.dot(
        chosen.astype(jnp.float32).astype(jnp.bfloat16),
        earlier.astype(jnp.bfloat16),
        preferred_element_type=jnp.float32,
    )
    place = jnp.where(chosen, before, -1.0).astype(jnp.int32)
    slot = lax.broadcasted_iota(jnp.int32, (CAPACITY, rows), 0)
    copies = []
    for j in range(EXPERTS):
        select = (place[j : j + 1] == slot).astype(jnp.float32).astype(jnp.bfloat16)
        start = 0
        for value_ref in values:
            width = value_ref.shape[2]
            buffer[j, :, start : start + width] = jnp.dot(
                select, value_ref[0], preferred_element_type=jnp.float32
            ).astype(jnp.bfloat16)
            start += width
        for i in range(out.shape[0]):
            for k in range(out.shape[2]):
                copy = pltpu.make_async_copy(
                    buffer.at[j], out.at[i, j, k], semaphores.at[len(copies)]
                )
                copy.start()
                copies.append(copy)
    for copy in copies:
        copy.wait()


def pick(step, plan, routes, values, n_xhi, per_expert):
    width = sum(value.shape[2] for value, _ in values)
    specs = [pl.BlockSpec((1,) + routes.shape[1:], lambda i, p: (p[step], 0, 0))]
    for value, planned in values:
        if planned:
            specs.append(pl.BlockSpec((1,) + value.shape[1:], lambda i, p: (p[step], 0, 0)))
        else:
            specs.append(pl.BlockSpec((1,) + value.shape[1:], lambda i, p: (0, 0, 0)))
    out = pl.pallas_call(
        pick_kernel,
        out_shape=jax.ShapeDtypeStruct(
            (n_xhi, EXPERTS, per_expert, CAPACITY, width), jnp.bfloat16
        ),
        grid_spec=pltpu.PrefetchScalarGridSpec(
            num_scalar_prefetch=1,
            grid=(1,),
            in_specs=specs,
            out_specs=pl.BlockSpec(memory_space=pltpu.HBM),
            scratch_shapes=[
                pltpu.VMEM((EXPERTS, CAPACITY, width), jnp.bfloat16),
                pltpu.SemaphoreType.DMA((n_xhi * EXPERTS * per_expert,)),
            ],
        ),
        compiler_params=pltpu.CompilerParams(dimension_semantics=("arbitrary",)),
        name="pick",
    )(plan, routes, *[value for value, _ in values])
    return out.reshape(n_xhi * EXPERTS * per_expert, CAPACITY, width)


def landed(value):
    anywhere = pl.BlockSpec(memory_space=pltpu.HBM)
    return pl.pallas_call(
        lambda value_ref, same_ref: None,
        out_shape=jax.ShapeDtypeStruct(value.shape, value.dtype),
        in_specs=[anywhere],
        out_specs=anywhere,
        input_output_aliases={0: 0},
        cost_estimate=pl.CostEstimate(
            flops=10**11, transcendentals=0, bytes_accessed=10**8
        ),
        name="landed",
    )(value)


def slots(route_now, share_now):
    rows = route_now.shape[0]
    named = route_now.T[None] == jnp.arange(EXPERTS, dtype=jnp.int32)[:, None, None]
    chosen = jnp.any(named, axis=1)
    mix = jnp.sum(jnp.where(named, share_now.T[None], 0.0), axis=1)
    token = jnp.arange(rows, dtype=jnp.int32)
    earlier = (token[:, None] < token[None, :]).astype(jnp.bfloat16)
    before = jnp.dot(
        chosen.astype(jnp.bfloat16), earlier, preferred_element_type=jnp.float32
    ).astype(jnp.int32)
    place = jnp.where(chosen, before, -1)
    hit = place[:, None, :] == jnp.arange(CAPACITY, dtype=jnp.int32)[None, :, None]
    mixing = jnp.where(hit, mix[:, None, :], 0.0).reshape(EXPERTS * CAPACITY, rows)
    return hit, mixing


def per_device(grad_in, saved_input, routes, route_weights, plan, up_weight, down_weight):
    n_expert = lax.axis_size("expert")
    n_xhi = lax.axis_size("xhi")
    n_section = lax.axis_size("section")
    per_expert = n_expert // EXPERTS
    peers = n_xhi * n_expert
    rows, quarter = grad_in.shape[1:]
    up_near = up_weight[0]
    up_far = pltpu.with_memory_space_constraint(up_near, pltpu.HBM)
    down_far = pltpu.with_memory_space_constraint(down_weight[0], pltpu.HBM)
    core = lax.axis_index("core").astype(jnp.int32).reshape(1)

    def swap_cores(value):
        return lax.ppermute(value, "core", [(0, 1), (1, 0)])

    def exchange(value):
        return lax.all_to_all(value, ("xhi", "expert"), split_axis=0, concat_axis=0, tiled=True)

    def deliver(sent):
        return exchange(sent).reshape(n_xhi, n_expert * CAPACITY, sent.shape[2])

    def combine(current, mixing, arrived):
        summed = jnp.sum(
            arrived.reshape(n_xhi, EXPERTS, per_expert, CAPACITY, quarter).astype(jnp.float32),
            axis=(0, 2),
        )
        moe_term = lax.dot_general(
            mixing,
            summed.reshape(EXPERTS * CAPACITY, quarter),
            (((0,), (0,)), ((), ())),
            precision=lax.Precision.HIGHEST,
            preferred_element_type=jnp.float32,
        )
        result = (current.astype(jnp.float32) + moe_term).astype(jnp.bfloat16)
        return lax.ppermute(
            result, "section", [(i, (i - 1) % n_section) for i in range(n_section)]
        )

    def outgoing(send, keep):
        return (
            keep.astype(jnp.float32) + swap_cores(send).astype(jnp.float32)
        ).astype(jnp.bfloat16).reshape(peers, CAPACITY, quarter)

    micros = plan[0]
    routes_by_choice = routes[0].transpose(0, 2, 1)
    saved_all = saved_input[0]
    current = grad_in[0]
    ticks = micros.shape[0]

    def slots_of(tick):
        route_now = lax.dynamic_index_in_dim(routes[0], micros[tick], 0, keepdims=False)
        share_now = lax.dynamic_index_in_dim(route_weights[0], micros[tick], 0, keepdims=False)
        return slots(route_now, share_now)

    def pick_rows(tick, *values):
        return pick(tick, micros, routes_by_choice, values, n_xhi, per_expert)

    both = deliver(pick_rows(0, (saved_all, True), (current[None], False)))
    later = None
    if ticks > 1:
        saved_sent, both = together(pick_rows(1, (saved_all, True)), both)
        later = deliver(saved_sent)
    swapped = swap_cores(both)
    factors = factor(core, (both, swapped, 0), up_far)
    send, keep = branch(core, (both, swapped, 1), up_near, down_far, factors)
    for tick in range(ticks):
        got = swap_cores(send)
        if tick + 1 < ticks:
            keep, later = together(keep, landed(later))
        partial_rows = (keep.astype(jnp.float32) + got.astype(jnp.float32)).astype(jnp.bfloat16)
        arrived = exchange(partial_rows.reshape(peers, CAPACITY, quarter))
        _, mixing = slots_of(tick)
        if tick + 1 == ticks:
            return combine(current, mixing, arrived)[None]
        later_swapped = pltpu.with_memory_space_constraint(swap_cores(later), pltpu.HBM)
        hit, _ = slots_of(tick + 1)
        picks = jnp.broadcast_to(
            hit[None, :, None], (n_xhi, EXPERTS, per_expert, CAPACITY, rows)
        ).reshape(peers * CAPACITY, rows)
        arrived, later_swapped, picks = together(arrived, later_swapped, picks)
        current = combine(current, mixing, arrived)
        grad_sent = jnp.dot(
            picks.astype(jnp.bfloat16), current, preferred_element_type=jnp.float32
        ).astype(jnp.bfloat16)
        grad_sent, later, later_swapped = together(
            grad_sent.reshape(peers, CAPACITY, quarter), later, later_swapped
        )
        grad_rows = deliver(grad_sent)
        factors = factor(core, (later, later_swapped, 0), up_far)
        grad_rows, factors = together(grad_rows, factors)
        swapped = swap_cores(grad_rows)
        own = own_act(core, grad_rows, down_far)
        grad_pre, send = sent_part(core, swapped, up_far, down_far, own, factors)
        keep = kept_part(core, up_far, grad_pre, send.shape)


def solution(mesh):
    sections, experts, parts = (mesh.shape[name] for name in ("section", "expert", "mp"))
    refined = Mesh(
        mesh.devices.reshape(sections, experts, parts // 2, 2),
        ("section", "expert", "xhi", "core"),
    )
    mp = ("xhi", "core")
    placed = (
        P("section", "expert", mp),
        P("section", None, "expert", mp),
        P("section", None, "expert", None),
        P("section", None, "expert", None),
        P("section", None),
        P("section", None, ("expert", "xhi", "core")),
        P("section", ("expert", "xhi", "core"), None),
    )
    return jax.shard_map(
        per_device,
        mesh=refined,
        in_specs=placed,
        out_specs=P("section", "expert", mp),
        check_vma=False,
    )
```

```python
import jax
import jax.numpy as jnp
from jax import lax
from jax.experimental import pallas as pl
from jax.experimental.pallas import tpu as pltpu
from jax.sharding import Mesh, PartitionSpec as P

EXPERTS = 4
CAPACITY = 72
HIDDEN_BLOCK = 256
VMEM_LIMIT = 22 * 1024 * 1024


def together(*values):
    return lax.optimization_barrier(values)


def contract_last(left, right):
    return lax.dot_general(
        left, right, (((1,), (1,)), ((), ())), preferred_element_type=jnp.float32
    )


HBM_SPEC = pl.BlockSpec(memory_space=pltpu.HBM)
VMEM_SPEC = pl.BlockSpec(memory_space=pltpu.VMEM)


def local_kernel(kernel, name, core, far, near, outs, scratch, flops=1000):
    return pl.pallas_call(
        kernel,
        out_shape=tuple(shape for shape, _ in outs),
        in_specs=[pl.BlockSpec(memory_space=pltpu.SMEM)]
        + [HBM_SPEC] * len(far)
        + [VMEM_SPEC] * len(near),
        out_specs=tuple(place for _, place in outs),
        scratch_shapes=scratch,
        compiler_params=pltpu.CompilerParams(vmem_limit_bytes=VMEM_LIMIT),
        cost_estimate=pl.CostEstimate(flops=flops, transcendentals=0, bytes_accessed=1000),
        name=name,
    )(core, *far, *near)


def row_copies(sources, column, rows_buf, semaphores):
    quarter = rows_buf.shape[2]
    halves = sources[0].shape[0]
    copies = [
        pltpu.make_async_copy(
            source.at[xhi, :, pl.ds(column * quarter, quarter)],
            rows_buf.at[n * halves + xhi],
            semaphores.at[n * halves + xhi],
        )
        for n, source in enumerate(sources)
        for xhi in range(halves)
    ]
    for copy in copies:
        copy.start()
    return copies


def first_feature(number, halves, core, quarter):
    side = core if number < halves else 1 - core
    return pl.multiple_of((2 * (number % halves) + side) * quarter, quarter)


def hidden_blocks(hidden):
    return [slice(start, start + HIDDEN_BLOCK) for start in range(0, hidden, HIDDEN_BLOCK)]


def factor_kernel(column, core_ref, mine, other, up, out, rows_buf, up_buf, semaphores):
    pieces, _, quarter = rows_buf.shape
    copies = row_copies((mine, other), column, rows_buf, semaphores)
    for number in range(pieces):
        first = first_feature(number, pieces // 2, core_ref[0], quarter)
        copies.append(
            pltpu.make_async_copy(
                up.at[pl.ds(first, quarter), :], up_buf.at[number], semaphores.at[pieces + number]
            )
        )
        copies[-1].start()
    for number in range(pieces):
        copies[number].wait()
        copies[pieces + number].wait()
        for block in hidden_blocks(up.shape[1]):
            part = jnp.dot(
                rows_buf[number], up_buf[number, :, block], preferred_element_type=jnp.float32
            )
            if number:
                part = out[:, block] + part
            if number + 1 == pieces:
                sigma = jax.nn.sigmoid(part)
                part = sigma * (1.0 + part * (1.0 - sigma))
            out[:, block] = part


def factor(core, saved, up):
    mine, other, column = saved
    halves, rows = mine.shape[:2]
    width, hidden = up.shape
    pieces = 2 * halves
    return local_kernel(
        lambda *refs: factor_kernel(column, *refs),
        "factor",
        core,
        [mine, other, up],
        [],
        [(pltpu.VMEM((rows, hidden), jnp.float32), VMEM_SPEC)],
        [
            pltpu.VMEM((pieces, rows, width // pieces), jnp.bfloat16),
            pltpu.VMEM((pieces, width // pieces, hidden), jnp.bfloat16),
            pltpu.SemaphoreType.DMA((2 * pieces,)),
        ],
    )[0]


def act_sums(sources, column, numbers, core, down, rows_buf, down_buf, semaphores):
    quarter = rows_buf.shape[2]
    copies = row_copies(sources, column, rows_buf, semaphores)
    count = len(numbers)
    for slot, number in enumerate(numbers):
        first = first_feature(number, sources[0].shape[0], core, quarter)
        copies.append(
            pltpu.make_async_copy(
                down.at[:, pl.ds(first, quarter)],
                down_buf.at[slot],
                semaphores.at[count + slot],
            )
        )
        copies[-1].start()
    for slot in range(count):
        copies[slot].wait()
        copies[count + slot].wait()
        for block in hidden_blocks(down.shape[0]):
            yield slot, block, contract_last(rows_buf[slot], down_buf[slot, block, :])


def up_copies(up, numbers, core, up_buf, semaphores):
    quarter = up_buf.shape[1]
    copies = []
    for slot, number in enumerate(numbers):
        first = first_feature(number, up.shape[0] // quarter // 2, core, quarter)
        copies.append(
            pltpu.make_async_copy(
                up.at[pl.ds(first, quarter), :], up_buf.at[slot], semaphores.at[slot]
            )
        )
        copies[-1].start()
    return copies


def loaded_parts(copies, grad_pre, up_buf, results, targets, semaphores):
    sent = []
    for slot, copy in enumerate(copies):
        copy.wait()
        results[slot] = contract_last(grad_pre[...], up_buf[slot]).astype(jnp.bfloat16)
        sent.append(
            pltpu.make_async_copy(results.at[slot], targets[slot], semaphores.at[slot])
        )
        sent[-1].start()
    for copy in sent:
        copy.wait()


def branch_parts(numbers, core, grad_pre, up, results, targets, semaphores):
    quarter = results.shape[2]
    halves = up.shape[0] // quarter // 2
    sent = []
    for slot, number in enumerate(numbers):
        first = first_feature(number, halves, core, quarter)
        results[slot] = contract_last(
            grad_pre[...], up[pl.ds(first, quarter), :]
        ).astype(jnp.bfloat16)
        copy = pltpu.make_async_copy(results.at[slot], targets[slot], semaphores.at[slot])
        copy.start()
        sent.append(copy)
    for copy in sent:
        copy.wait()


def branch_kernel(
    column, core_ref, mine, other, down, up, factors, send, keep, rows_buf, down_buf, acc,
    grad_pre, results, semaphores, out_semaphores,
):
    pieces = rows_buf.shape[0]
    halves = pieces // 2
    for slot, block, part in act_sums(
        (mine, other), column, range(pieces), core_ref[0], down, rows_buf, down_buf, semaphores
    ):
        total = acc[:, block] + part if slot else part
        if slot + 1 < pieces:
            acc[:, block] = total
        else:
            grad_pre[:, block] = (total * factors[:, block]).astype(jnp.bfloat16)
    numbers = [halves + n for n in range(halves)] + list(range(halves))
    targets = [send.at[n] for n in range(halves)] + [keep.at[n] for n in range(halves)]
    branch_parts(numbers, core_ref[0], grad_pre, up, results, targets, out_semaphores)


def act_buffers(pieces, rows, quarter, hidden):
    return [
        pltpu.VMEM((pieces, rows, quarter), jnp.bfloat16),
        pltpu.VMEM((pieces, hidden, quarter), jnp.bfloat16),
    ]


def branch(core, grads, up, down, factors):
    mine, other, column = grads
    halves, rows = mine.shape[:2]
    hidden, width = down.shape
    pieces = 2 * halves
    quarter = width // pieces
    part = (halves, rows, quarter)
    return local_kernel(
        lambda *refs: branch_kernel(column, *refs),
        "branch",
        core,
        [mine, other, down],
        [up, factors],
        [
            (jax.ShapeDtypeStruct(part, jnp.bfloat16), HBM_SPEC),
            (pltpu.HBM(part, jnp.bfloat16), HBM_SPEC),
        ],
        act_buffers(pieces, rows, quarter, hidden)
        + [
            pltpu.VMEM((rows, hidden), jnp.float32),
            pltpu.VMEM((rows, hidden), jnp.bfloat16),
            pltpu.VMEM((pieces, rows, quarter), jnp.bfloat16),
            pltpu.SemaphoreType.DMA((2 * pieces,)),
            pltpu.SemaphoreType.DMA((pieces,)),
        ],
    )


def own_act_kernel(core_ref, mine, down, out, rows_buf, down_buf, semaphores):
    for slot, block, part in act_sums(
        (mine,), 0, range(mine.shape[0]), core_ref[0], down, rows_buf, down_buf, semaphores
    ):
        out[:, block] = out[:, block] + part if slot else part


def own_act(core, mine, down):
    halves, rows, quarter = mine.shape
    return local_kernel(
        own_act_kernel,
        "own_act",
        core,
        [mine, down],
        [],
        [(pltpu.VMEM((rows, down.shape[0]), jnp.float32), VMEM_SPEC)],
        act_buffers(halves, rows, quarter, down.shape[0])
        + [pltpu.SemaphoreType.DMA((2 * halves,))],
    )[0]


def sent_kernel(
    core_ref, other, down, up, own, factors, grad_pre, send, rows_buf, down_buf, up_buf, acc,
    results, semaphores, up_semaphores, out_semaphores,
):
    halves = rows_buf.shape[0]
    late = [halves + n for n in range(halves)]
    copies = None
    for slot, block, part in act_sums(
        (other,), 0, late, core_ref[0], down, rows_buf, down_buf, semaphores
    ):
        if copies is None:
            copies = up_copies(up, late, core_ref[0], up_buf, up_semaphores)
        total = (acc if slot else own)[:, block] + part
        if slot + 1 < halves:
            acc[:, block] = total
        else:
            grad_pre[:, block] = (total * factors[:, block]).astype(jnp.bfloat16)
    targets = [send.at[n] for n in range(halves)]
    loaded_parts(copies, grad_pre, up_buf, results, targets, out_semaphores)


def sent_part(core, other, up, down, own, factors):
    halves, rows, quarter = other.shape
    hidden = down.shape[0]
    return local_kernel(
        sent_kernel,
        "sent_part",
        core,
        [other, down, up],
        [own, factors],
        [
            (pltpu.VMEM((rows, hidden), jnp.bfloat16), VMEM_SPEC),
            (jax.ShapeDtypeStruct(other.shape, jnp.bfloat16), HBM_SPEC),
        ],
        act_buffers(halves, rows, quarter, hidden)
        + [
            pltpu.VMEM((halves, quarter, hidden), jnp.bfloat16),
            pltpu.VMEM((rows, hidden), jnp.float32),
            pltpu.VMEM((halves, rows, quarter), jnp.bfloat16),
            pltpu.SemaphoreType.DMA((2 * halves,)),
            pltpu.SemaphoreType.DMA((halves,)),
            pltpu.SemaphoreType.DMA((halves,)),
        ],
    )


def kept_kernel(core_ref, up, grad_pre, keep, up_buf, results, up_semaphores, semaphores):
    halves = keep.shape[0]
    copies = up_copies(up, range(halves), core_ref[0], up_buf, up_semaphores)
    targets = [keep.at[n] for n in range(halves)]
    loaded_parts(copies, grad_pre, up_buf, results, targets, semaphores)


def kept_part(core, up, grad_pre, part):
    return local_kernel(
        kept_kernel,
        "kept_part",
        core,
        [up],
        [grad_pre],
        [(jax.ShapeDtypeStruct(part, jnp.bfloat16), HBM_SPEC)],
        [
            pltpu.VMEM((part[0], part[2], up.shape[1]), jnp.bfloat16),
            pltpu.VMEM(part, jnp.bfloat16),
            pltpu.SemaphoreType.DMA((part[0],)),
            pltpu.SemaphoreType.DMA((part[0],)),
        ],
        flops=10**10,
    )[0]


def pick_kernel(plan_ref, routes_ref, *refs):
    del plan_ref
    values, (out, buffer, semaphores) = refs[:-3], refs[-3:]
    rows = routes_ref.shape[2]
    expert = lax.broadcasted_iota(jnp.int32, (16, rows), 0)
    named = routes_ref[0]
    chosen = named[0:1] == expert
    for choice in range(1, named.shape[0]):
        chosen = chosen | (named[choice : choice + 1] == expert)
    earlier = (
        lax.broadcasted_iota(jnp.int32, (rows, rows), 0)
        < lax.broadcasted_iota(jnp.int32, (rows, rows), 1)
    ).astype(jnp.float32)
    before = jnp.dot(
        chosen.astype(jnp.float32).astype(jnp.bfloat16),
        earlier.astype(jnp.bfloat16),
        preferred_element_type=jnp.float32,
    )
    place = jnp.where(chosen, before, -1.0).astype(jnp.int32)
    slot = lax.broadcasted_iota(jnp.int32, (CAPACITY, rows), 0)
    copies = []
    for j in range(EXPERTS):
        select = (place[j : j + 1] == slot).astype(jnp.float32).astype(jnp.bfloat16)
        start = 0
        for value_ref in values:
            width = value_ref.shape[2]
            buffer[j, :, start : start + width] = jnp.dot(
                select, value_ref[0], preferred_element_type=jnp.float32
            ).astype(jnp.bfloat16)
            start += width
        for i in range(out.shape[0]):
            for k in range(out.shape[2]):
                copy = pltpu.make_async_copy(
                    buffer.at[j], out.at[i, j, k], semaphores.at[len(copies)]
                )
                copy.start()
                copies.append(copy)
    for copy in copies:
        copy.wait()


def pick(step, plan, routes, values, n_xhi, per_expert):
    width = sum(value.shape[2] for value, _ in values)
    specs = [pl.BlockSpec((1,) + routes.shape[1:], lambda i, p: (p[step], 0, 0))]
    for value, planned in values:
        if planned:
            specs.append(pl.BlockSpec((1,) + value.shape[1:], lambda i, p: (p[step], 0, 0)))
        else:
            specs.append(pl.BlockSpec((1,) + value.shape[1:], lambda i, p: (0, 0, 0)))
    out = pl.pallas_call(
        pick_kernel,
        out_shape=jax.ShapeDtypeStruct(
            (n_xhi, EXPERTS, per_expert, CAPACITY, width), jnp.bfloat16
        ),
        grid_spec=pltpu.PrefetchScalarGridSpec(
            num_scalar_prefetch=1,
            grid=(1,),
            in_specs=specs,
            out_specs=pl.BlockSpec(memory_space=pltpu.HBM),
            scratch_shapes=[
                pltpu.VMEM((EXPERTS, CAPACITY, width), jnp.bfloat16),
                pltpu.SemaphoreType.DMA((n_xhi * EXPERTS * per_expert,)),
            ],
        ),
        compiler_params=pltpu.CompilerParams(dimension_semantics=("arbitrary",)),
        name="pick",
    )(plan, routes, *[value for value, _ in values])
    return out.reshape(n_xhi * EXPERTS * per_expert, CAPACITY, width)


def landed(value):
    anywhere = pl.BlockSpec(memory_space=pltpu.HBM)
    return pl.pallas_call(
        lambda value_ref, same_ref: None,
        out_shape=jax.ShapeDtypeStruct(value.shape, value.dtype),
        in_specs=[anywhere],
        out_specs=anywhere,
        input_output_aliases={0: 0},
        cost_estimate=pl.CostEstimate(
            flops=10**11, transcendentals=0, bytes_accessed=10**8
        ),
        name="landed",
    )(value)


def slots(route_now, share_now):
    rows = route_now.shape[0]
    named = route_now.T[None] == jnp.arange(EXPERTS, dtype=jnp.int32)[:, None, None]
    chosen = jnp.any(named, axis=1)
    mix = jnp.sum(jnp.where(named, share_now.T[None], 0.0), axis=1)
    token = jnp.arange(rows, dtype=jnp.int32)
    earlier = (token[:, None] < token[None, :]).astype(jnp.bfloat16)
    before = jnp.dot(
        chosen.astype(jnp.bfloat16), earlier, preferred_element_type=jnp.float32
    ).astype(jnp.int32)
    place = jnp.where(chosen, before, -1)
    hit = place[:, None, :] == jnp.arange(CAPACITY, dtype=jnp.int32)[None, :, None]
    mixing = jnp.where(hit, mix[:, None, :], 0.0).reshape(EXPERTS * CAPACITY, rows)
    return hit, mixing


def per_device(grad_in, saved_input, routes, route_weights, plan, up_weight, down_weight):
    n_expert = lax.axis_size("expert")
    n_xhi = lax.axis_size("xhi")
    n_section = lax.axis_size("section")
    per_expert = n_expert // EXPERTS
    peers = n_xhi * n_expert
    rows, quarter = grad_in.shape[1:]
    up_near = up_weight[0]
    up_far = pltpu.with_memory_space_constraint(up_near, pltpu.HBM)
    down_far = pltpu.with_memory_space_constraint(down_weight[0], pltpu.HBM)
    core = lax.axis_index("core").astype(jnp.int32).reshape(1)

    def swap_cores(value):
        return lax.ppermute(value, "core", [(0, 1), (1, 0)])

    def exchange(value):
        return lax.all_to_all(value, ("xhi", "expert"), split_axis=0, concat_axis=0, tiled=True)

    def deliver(sent):
        return exchange(sent).reshape(n_xhi, n_expert * CAPACITY, sent.shape[2])

    def combine(current, mixing, arrived):
        summed = jnp.sum(
            arrived.reshape(n_xhi, EXPERTS, per_expert, CAPACITY, quarter).astype(jnp.float32),
            axis=(0, 2),
        )
        moe_term = lax.dot_general(
            mixing,
            summed.reshape(EXPERTS * CAPACITY, quarter),
            (((0,), (0,)), ((), ())),
            precision=lax.Precision.HIGHEST,
            preferred_element_type=jnp.float32,
        )
        result = (current.astype(jnp.float32) + moe_term).astype(jnp.bfloat16)
        return lax.ppermute(
            result, "section", [(i, (i - 1) % n_section) for i in range(n_section)]
        )

    def outgoing(send, keep):
        return (
            keep.astype(jnp.float32) + swap_cores(send).astype(jnp.float32)
        ).astype(jnp.bfloat16).reshape(peers, CAPACITY, quarter)

    micros = plan[0]
    routes_by_choice = routes[0].transpose(0, 2, 1)
    saved_all = saved_input[0]
    current = grad_in[0]
    ticks = micros.shape[0]

    def slots_of(tick):
        route_now = lax.dynamic_index_in_dim(routes[0], micros[tick], 0, keepdims=False)
        share_now = lax.dynamic_index_in_dim(route_weights[0], micros[tick], 0, keepdims=False)
        return slots(route_now, share_now)

    def pick_rows(tick, *values):
        return pick(tick, micros, routes_by_choice, values, n_xhi, per_expert)

    both = deliver(pick_rows(0, (saved_all, True), (current[None], False)))
    later = None
    if ticks > 1:
        saved_sent, both = together(pick_rows(1, (saved_all, True)), both)
        later = deliver(saved_sent)
    swapped = swap_cores(both)
    factors = factor(core, (both, swapped, 0), up_far)
    send, keep = branch(core, (both, swapped, 1), up_near, down_far, factors)
    for tick in range(ticks):
        got = swap_cores(send)
        if tick + 1 < ticks:
            keep, later = together(keep, landed(later))
        partial_rows = (keep.astype(jnp.float32) + got.astype(jnp.float32)).astype(jnp.bfloat16)
        partial_rows = partial_rows.reshape(peers, CAPACITY, quarter)
        if tick + 1 < ticks:
            partial_rows, later = together(partial_rows, later)
        arrived = exchange(partial_rows)
        _, mixing = slots_of(tick)
        if tick + 1 == ticks:
            return combine(current, mixing, arrived)[None]
        later_swapped = pltpu.with_memory_space_constraint(swap_cores(later), pltpu.HBM)
        hit, _ = slots_of(tick + 1)
        picks = jnp.broadcast_to(
            hit[None, :, None], (n_xhi, EXPERTS, per_expert, CAPACITY, rows)
        ).reshape(peers * CAPACITY, rows)
        arrived, later_swapped, picks = together(arrived, later_swapped, picks)
        current = combine(current, mixing, arrived)
        grad_sent = jnp.dot(
            picks.astype(jnp.bfloat16), current, preferred_element_type=jnp.float32
        ).astype(jnp.bfloat16)
        grad_sent, later, later_swapped = together(
            grad_sent.reshape(peers, CAPACITY, quarter), later, later_swapped
        )
        grad_rows = deliver(grad_sent)
        factors = factor(core, (later, later_swapped, 0), up_far)
        grad_rows, factors = together(grad_rows, factors)
        swapped = swap_cores(grad_rows)
        own = own_act(core, grad_rows, down_far)
        grad_pre, send = sent_part(core, swapped, up_far, down_far, own, factors)
        keep = kept_part(core, up_far, grad_pre, send.shape)


def solution(mesh):
    sections, experts, parts = (mesh.shape[name] for name in ("section", "expert", "mp"))
    refined = Mesh(
        mesh.devices.reshape(sections, experts, parts // 2, 2),
        ("section", "expert", "xhi", "core"),
    )
    mp = ("xhi", "core")
    placed = (
        P("section", "expert", mp),
        P("section", None, "expert", mp),
        P("section", None, "expert", None),
        P("section", None, "expert", None),
        P("section", None),
        P("section", None, ("expert", "xhi", "core")),
        P("section", ("expert", "xhi", "core"), None),
    )
    return jax.shard_map(
        per_device,
        mesh=refined,
        in_specs=placed,
        out_specs=P("section", "expert", mp),
        check_vma=False,
    )
```
